128 devices in a mesh: tm: 8 (over y, x_hi), agent: 16 (over z, x_lo, core).
Axes of the slice: x: 4 (x_hi: 2, x_lo: 2; x = x_hi * 2 + x_lo), y: 4, z: 4, core: 2. Of those that a mesh axis runs over, the one named last changes fastest.
Arguments:
- tokens: bfloat16 [32, 1024, 1024], P('tm', 'agent'), may hold values from -6 to 6
- conv_taps: float32 [5, 1024], replicated, may hold values from -3 to 3
- norm_first: float32 [1024], replicated, may hold values from 0.1 to 1.9
- norm_second: float32 [1024], replicated, may hold values from 0.1 to 1.9
- norm_third: float32 [1024], replicated, may hold values from 0.1 to 1.9
- w_in: bfloat16 [1024, 3072], replicated, may hold values from -0.1875 to 0.1875
- w_out: bfloat16 [3072, 1024], replicated, may hold values from -0.109375 to 0.109375
- w_query: bfloat16 [1024, 1024], replicated, may hold values from -16 to 16
- w_key: bfloat16 [1024, 1024], replicated, may hold values from -16 to 16
- w_value: bfloat16 [1024, 1024], replicated, may hold values from -0.1875 to 0.1875
- w_output: bfloat16 [1024, 1024], replicated, may hold values from -0.1875 to 0.1875
- agent_order: int32 [1024], P('agent'), may hold values from 0 to 1023, each once
- present_steps: int32 [1024], P('agent'), may hold values from 1 to 32
Outputs:
- result: bfloat16 [32, 1024, 1024], P('tm', 'agent')
The draws below stay inside these ranges and needn't reach their ends.
Inputs may be any that keep to these rules, and one draw needn't show every extreme that they name: `agent_order`: each of 0 to 1023 appears once.
All inputs are finite; a program needn't handle non-finite values.
Results may differ from the reference program's by a relative error of at most 0.012.
Values may be sent and summed in bfloat16 or wider, within the bound.
A program may use at most 192 MiB of HBM per device.

```python
import jax
import jax.numpy as jnp
from jax import lax

D = 1024
HEADS = 16
FF = 3072
KERNEL = 5
HEAD = 64
STEPS = 32
AGENTS = 1024


def shared_base(key):
    return jax.random.normal(jax.random.fold_in(key, 101), (D, D), jnp.float32) * D ** (-0.5)


def draw_w_query(key, part):
    extra = jax.random.normal(jax.random.fold_in(key, 102), (D, D), jnp.float32) * D ** (-0.5)
    return (shared_base(key) + 0.7 * extra).astype(jnp.bfloat16)


def draw_w_key(key, part):
    extra = jax.random.normal(jax.random.fold_in(key, 103), (D, D), jnp.float32) * D ** (-0.5)
    return (1.2 * extra).astype(jnp.bfloat16)


def set_ends(array, own_key, smallest, high):
    longest = array.shape.index(max(array.shape))
    spots = []
    for shift in (0, 1):
        where = [jax.random.randint(jax.random.fold_in(own_key, axis), (), 0, length) for axis, length in enumerate(array.shape)]
        where[longest] = (where[longest] + shift) % array.shape[longest]
        spots.append(tuple(where))
    return array.at[spots[0]].set(smallest).at[spots[1]].set(high)


def levels(stream_key, extent, pieces, least, high):
    level, own = 1.0, jax.random.fold_in(stream_key, 6)
    for position, blocks in pieces:
        draws = jnp.exp(jax.random.uniform(jax.random.fold_in(own, position), (blocks,), jnp.float32, least / len(pieces), high / len(pieces)))
        level = level * jnp.repeat(draws, extent[position] // blocks).reshape([-1 if axis == position else 1 for axis in range(len(extent))])
    return level


def centred(key, dims, spread, most, pieces=(), held_as=jnp.bfloat16):
    drawn = spread * jax.random.normal(key, dims, jnp.float32)
    if pieces:
        drawn = drawn * levels(key, dims, pieces, -0.22, 0.18)
    return jnp.clip(drawn, -most, most).astype(held_as)


def setup_inputs(seed: int = 0) -> dict:
    splits = jax.random.split(jax.random.key(seed), 14)
    return {
        "tokens": centred(splits[0], (STEPS, AGENTS, D), 1.0, 6.0, ((0, 8), (1, 16))),
        "conv_taps": centred(splits[1], (KERNEL, D), 0.5, 3.0, (), jnp.float32),
        "norm_first": jnp.clip(1.0 + 0.18 * jax.random.normal(splits[2], (D,), jnp.float32), 0.1, 1.9),
        "norm_second": jnp.clip(1.0 + 0.18 * jax.random.normal(splits[3], (D,), jnp.float32), 0.1, 1.9),
        "norm_third": jnp.clip(1.0 + 0.18 * jax.random.normal(splits[4], (D,), jnp.float32), 0.1, 1.9),
        "w_in": centred(splits[5], (D, FF), D ** -0.5, 0.1875),
        "w_out": centred(splits[6], (FF, D), FF ** -0.5, 0.109375),
        "w_query": draw_w_query(jax.random.fold_in(splits[13], 71), 0),
        "w_key": draw_w_key(jax.random.fold_in(splits[13], 71), 0),
        "w_value": centred(splits[9], (D, D), D ** -0.5, 0.1875),
        "w_output": centred(splits[10], (D, D), D ** -0.5, 0.1875),
        "agent_order": jax.random.permutation(splits[11], AGENTS).astype(jnp.int32),
        "present_steps": set_ends(jax.random.randint(splits[12], (AGENTS,), 1, STEPS + 1), jax.random.fold_in(splits[12], 1), 1, STEPS).astype(jnp.int32),
    }


EPS = 1e-05

def normed_rows(rows, gain):
    values = rows.astype(jnp.float32)
    scale = lax.rsqrt(lax.optimization_barrier(jnp.mean(values * values, axis=-1, keepdims=True)) + EPS)
    return values * scale * gain.astype(jnp.float32)

def reference(tokens, conv_taps, norm_first, norm_second, norm_third, w_in, w_out, w_query, w_key, w_value, w_output, agent_order, present_steps):
    reach = KERNEL - 1
    normed = normed_rows(tokens, norm_first)
    padded = jnp.pad(normed, ((reach, 0), (0, 0), (0, 0)))
    mixed = jnp.zeros(normed.shape, jnp.float32)
    for lag in range(KERNEL):
        mixed = mixed + conv_taps[lag].astype(jnp.float32) * padded[reach - lag:reach - lag + STEPS]
    first = (tokens.astype(jnp.float32) + mixed).astype(jnp.bfloat16)
    flat = first.reshape(STEPS * AGENTS, D)
    inner = normed_rows(flat, norm_second).astype(jnp.bfloat16)
    hidden = jax.nn.gelu(jnp.dot(inner, w_in, preferred_element_type=jnp.float32), approximate=False).astype(jnp.bfloat16)
    second = (flat.astype(jnp.float32) + jnp.dot(hidden, w_out, preferred_element_type=jnp.float32)).astype(jnp.bfloat16)
    attn_in = normed_rows(second, norm_third).astype(jnp.bfloat16)
    query = jnp.dot(attn_in, w_query, preferred_element_type=jnp.float32).astype(jnp.bfloat16).reshape(STEPS, AGENTS, HEADS, HEAD)
    keys = jnp.dot(attn_in, w_key, preferred_element_type=jnp.float32).astype(jnp.bfloat16).reshape(STEPS, AGENTS, HEADS, HEAD)
    values = jnp.dot(attn_in, w_value, preferred_element_type=jnp.float32).astype(jnp.bfloat16).reshape(STEPS, AGENTS, HEADS, HEAD)
    earlier = agent_order[None, :] < agent_order[:, None]
    itself = agent_order[None, :] == agent_order[:, None]
    scale = HEAD ** (-0.5)

    def one_step(item):
        step_query, step_keys, step_values, step = item
        scores = jnp.einsum('ahd,bhd->hab', step_query.astype(jnp.float32), step_keys.astype(jnp.float32)) * scale
        visible = earlier & (step < present_steps[None, :]) | itself
        masked = jnp.where(visible[None], scores, -1e+30)
        top = lax.optimization_barrier(jnp.max(masked, axis=-1, keepdims=True))
        weights = jnp.where(visible[None], jnp.exp(masked - top), 0.0).astype(jnp.bfloat16)
        total = lax.optimization_barrier(jnp.sum(weights.astype(jnp.float32), axis=-1))
        summed = jnp.einsum('hab,bhd->ahd', weights.astype(jnp.float32), step_values.astype(jnp.float32))
        return (summed / jnp.transpose(total)[:, :, None]).astype(jnp.bfloat16)
    attended = lax.map(one_step, (query, keys, values, jnp.arange(STEPS, dtype=jnp.int32)))
    attended = attended.reshape(STEPS * AGENTS, D)
    result = second.astype(jnp.float32) + jnp.dot(attended, w_output, preferred_element_type=jnp.float32)
    return result.astype(jnp.bfloat16).reshape(STEPS, AGENTS, D)
```

```python
import functools

import jax
import jax.numpy as jnp
from jax import lax
from jax.experimental import pallas as pl
from jax.experimental.pallas import tpu as pltpu
from jax.sharding import PartitionSpec as P

EPS = 1e-05
HEADS = 16
MESH = pl.DeviceIdType.MESH
F32, BF16 = jnp.float32, jnp.bfloat16
GROUP = 16
LAYERS = 4
ROWS = 64
WIDTH = 1024
HIDDEN = 3072
COLS = 256
FF_TILE = 512
BLOCKS = ((0, 1, 2, 3),)


def remote(src, dst, send, recv, tm, agent):
    return pltpu.make_async_remote_copy(
        src_ref=src,
        dst_ref=dst,
        send_sem=send,
        recv_sem=recv,
        device_id=(tm, agent),
        device_id_type=MESH,
    )


def normed(rows, gain):
    scale = lax.rsqrt(jnp.mean(rows * rows, axis=-1, keepdims=True) + EPS)
    return rows * scale * gain


def block_kernel(
    tokens,
    taps,
    gain_first,
    gain_second,
    gain_third,
    w_in,
    w_out,
    w_query,
    w_key,
    w_value,
    w_output,
    info_own,
    result,
    win_v,
    wout_v,
    wqkv_v,
    wo_v,
    tok_v,
    prev_v,
    norm_v,
    hid_v,
    second_v,
    mine_v,
    gath_v,
    query_v,
    key_v,
    value_v,
    att_v,
    back_v,
    info_v,
    okey_v,
    oquery_v,
    local_sem,
    shift_send,
    shift_recv,
    info_send,
    info_recv,
    ex_send,
    ex_recv,
    rel_send,
    rel_recv,
    ret_send,
    ret_recv,
):
    tm, me = lax.axis_index("tm"), lax.axis_index("agent")
    n_tm = lax.axis_size("tm")
    z, x, core = me // 4, lax.rem(me // 2, 2), lax.rem(me, 2)
    group = lax.rem(me, 4)
    sibling = me + 1 - 2 * core
    across = me + 2 - 4 * x
    after, before = lax.rem(tm + 1, n_tm), lax.rem(tm + n_tm - 1, n_tm)

    cols = pl.ds(pl.multiple_of(group * COLS, COLS), COLS)
    loads = [
        pltpu.make_async_copy(tokens, tok_v, local_sem.at[0]),
        pltpu.make_async_copy(w_in, win_v, local_sem.at[1]),
        pltpu.make_async_copy(w_out, wout_v, local_sem.at[2]),
        pltpu.make_async_copy(w_query.at[:, cols], wqkv_v.at[0], local_sem.at[3]),
        pltpu.make_async_copy(w_key.at[:, cols], wqkv_v.at[1], local_sem.at[4]),
        pltpu.make_async_copy(w_value.at[:, cols], wqkv_v.at[2], local_sem.at[5]),
        pltpu.make_async_copy(w_output, wo_v, local_sem.at[6]),
    ]
    for load in loads:
        load.start()

    barrier = pltpu.get_barrier_semaphore()

    def greet(d, carry):
        pl.semaphore_signal(
            barrier, inc=1, device_id=(tm, lax.rem(me + d, GROUP)), device_id_type=MESH
        )
        return carry

    pl.semaphore_signal(barrier, inc=1, device_id=(before, me), device_id_type=MESH)
    pl.semaphore_signal(barrier, inc=1, device_id=(after, me), device_id_type=MESH)
    lax.fori_loop(1, GROUP, greet, 0)
    pl.semaphore_wait(barrier, GROUP + 1)

    def shift(step):
        return remote(
            tokens.at[step],
            prev_v.at[step],
            shift_send.at[step],
            shift_recv.at[step],
            after,
            me,
        )

    order = (3, 2, 1, 0)

    @pl.when(tm < n_tm - 1)
    def _():
        for step in order:
            shift(step).start()

    @pl.when(tm == 0)
    def _():
        prev_v[...] = jnp.zeros_like(prev_v)

    def info_copy(slot, peer):
        return remote(
            info_own, info_v.at[slot], info_send.at[peer], info_recv.at[slot], tm, peer
        )

    def tell(d, carry):
        info_copy(me, lax.rem(me + d, GROUP)).start()
        return carry

    own_info = pltpu.make_async_copy(info_own, info_v.at[me], local_sem.at[7])
    own_info.start()
    lax.fori_loop(1, GROUP, tell, 0)

    gain1, gain2, gain3 = gain_first[...], gain_second[...], gain_third[...]
    loads[0].wait()
    for step in range(4):
        norm_v[4 + step] = normed(tok_v[step].astype(F32), gain1)
    arrived = set()
    local_pieces = []
    for number, block in enumerate(BLOCKS):
        for step in order:
            if step >= min(block) and step not in arrived:
                arrived.add(step)

                @pl.when(tm > 0)
                def _(step=step):
                    shift(step).wait_recv()

                norm_v[step] = normed(prev_v[step].astype(F32), gain1)
        rows = pl.ds(min(block) * ROWS, len(block) * ROWS)
        firsts = []
        for step in block:
            mixed = taps[0:1, :] * norm_v[step + 4]
            for lag in range(1, 5):
                mixed = mixed + taps[lag : lag + 1, :] * norm_v[step + 4 - lag]
            firsts.append((tok_v[step].astype(F32) + mixed).astype(BF16))
        first = jnp.concatenate(firsts, axis=0)
        second_v[rows, :] = first
        inner = normed(first.astype(F32), gain2).astype(BF16)
        if number == 0:
            loads[1].wait()
        for tile in range(0, HIDDEN, FF_TILE):
            pre = jnp.dot(inner, win_v[:, tile : tile + FF_TILE], preferred_element_type=F32)
            act = 0.5 * pre * (1.0 + lax.erf(pre * 0.7071067811865476))
            hid_v[rows, tile : tile + FF_TILE] = act.astype(BF16)
        if number == 0:
            loads[2].wait()
        ffn = jnp.dot(hid_v[rows, :], wout_v[...], preferred_element_type=F32)
        second = (second_v[rows, :].astype(F32) + ffn).astype(BF16)
        second_v[rows, :] = second
        attn_in = normed(second.astype(F32), gain3).astype(BF16)
        for spot, step in enumerate(block):
            mine_v[step] = attn_in[spot * ROWS : (spot + 1) * ROWS]

        for step in block:
            far = remote(
                mine_v.at[step],
                gath_v.at[me],
                ex_send.at[step * 2 + 1],
                ex_recv.at[me],
                tm,
                step * 4 + 2 * (1 - x) + core,
            )
            far.start()
            near = remote(
                mine_v.at[step],
                gath_v.at[me],
                ex_send.at[step * 2],
                ex_recv.at[me],
                tm,
                step * 4 + 2 * x + core,
            )

            @pl.when(z != step)
            def _(near=near):
                near.start()

            @pl.when(z == step)
            def _(step=step):
                pltpu.make_async_copy(
                    mine_v.at[step], gath_v.at[me], local_sem.at[8]
                ).start()
                remote(
                    mine_v.at[step],
                    gath_v.at[me],
                    rel_send.at[me],
                    rel_recv.at[me],
                    tm,
                    sibling,
                ).start()

    def arrive(slot, recv):
        remote(mine_v.at[0], gath_v.at[slot], ex_send.at[0], recv.at[slot], tm, me).wait_recv()

    def forward(slot):
        return remote(
            gath_v.at[slot],
            gath_v.at[slot],
            rel_send.at[slot],
            rel_recv.at[slot],
            tm,
            sibling,
        )

    own_info.wait()

    def heard(d, carry):
        peer = lax.rem(me + d, GROUP)
        info_copy(peer, peer).wait_recv()
        return carry

    lax.fori_loop(1, GROUP, heard, 0)
    now = tm * LAYERS + z
    low = lax.broadcasted_iota(jnp.int32, (1, 128), 1) < ROWS
    eye = lax.broadcasted_iota(jnp.int32, (128, 128), 0) == lax.broadcasted_iota(
        jnp.int32, (128, 128), 1
    )
    for pair in range(GROUP // 2):
        left, right = info_v[2 * pair], info_v[2 * pair + 1]
        place = jnp.where(low, left[0:1], right[0:1])
        until = jnp.where(low, left[1:2], right[1:2])
        place_f = place.astype(F32)
        span = slice(pair * 128, pair * 128 + 128)
        okey_v[0:1, span] = jnp.where(now < until, place_f, 1e9)
        oquery_v[span, :] = jnp.sum(
            jnp.where(eye, jnp.broadcast_to(place_f, (128, 128)), 0.0), axis=1, keepdims=True
        )

    for load in loads[3:6]:
        load.wait()
    lane = lax.broadcasted_iota(jnp.int32, (COLS, 128), 1) < 64

    def project(layer):
        rows = pl.ds(pl.multiple_of(layer * COLS, COLS), COLS)
        source = gath_v[pl.ds(layer * 4, 4)].reshape(COLS, WIDTH)
        query = jnp.dot(source, wqkv_v[0], preferred_element_type=F32) * 0.125
        key = jnp.dot(source, wqkv_v[1], preferred_element_type=F32)
        value = jnp.dot(source, wqkv_v[2], preferred_element_type=F32)
        for pair in range(2):
            span = slice(pair * 128, pair * 128 + 128)
            query_v[pair, rows, :] = query[:, span].astype(BF16)
            key_v[2 * pair, rows, :] = jnp.where(lane, key[:, span], 0.0).astype(BF16)
            key_v[2 * pair + 1, rows, :] = jnp.where(lane, 0.0, key[:, span]).astype(BF16)
            value_v[2 * pair, rows, :] = jnp.where(lane, value[:, span], 1.0).astype(BF16)
            value_v[2 * pair + 1, rows, :] = jnp.where(lane, 1.0, value[:, span]).astype(BF16)

    turns = (0, 1, 3, 2)

    def slots(turn):
        base = lax.rem(z + turn, LAYERS) * 4
        return base + 2 * x + core, base + 2 * (1 - x) + core

    def from_sibling(turn):
        for slot in slots(turn):
            arrive(slot + 1 - 2 * core, rel_recv)

    for index, turn in enumerate(turns):
        near, far = slots(turn)
        if turn:
            arrive(near, ex_recv)
            forward(near).start()
        arrive(far, ex_recv)
        forward(far).start()
        if turn == 0:
            pltpu.make_async_copy(mine_v.at[0], gath_v.at[me], local_sem.at[8]).wait()
        if index:
            from_sibling(turns[index - 1])
            project(lax.rem(z + turns[index - 1], LAYERS))
    from_sibling(turns[-1])
    project(lax.rem(z + turns[-1], LAYERS))

    home_cols = pl.ds(pl.multiple_of(group * COLS, COLS), COLS)

    def give(home):
        return remote(
            att_v.at[pl.ds(pl.multiple_of(home * ROWS, ROWS), ROWS), :],
            back_v.at[z, :, home_cols],
            ret_send.at[home],
            ret_recv.at[me],
            tm,
            home,
        )

    half = lax.broadcasted_iota(jnp.int32, (COLS, 128), 1) < 64

    def attend(index, carry):
        layer = lax.rem(z + 3 - index, LAYERS)
        start = pl.multiple_of(layer * COLS, COLS)
        rows = pl.ds(start, COLS)
        row = lax.broadcasted_iota(jnp.int32, (COLS, GROUP * ROWS), 0) + start
        column = lax.broadcasted_iota(jnp.int32, (COLS, GROUP * ROWS), 1)
        visible = (okey_v[0:1, :] < oquery_v[rows, :]) | (row == column)
        bias = jnp.where(visible, 0.0, -1e30)
        for pair in range(2):
            query = query_v[pair, rows, :]
            parts = []
            for head in (2 * pair, 2 * pair + 1):
                scores = lax.dot_general(
                    query,
                    key_v[head],
                    (((1,), (1,)), ((), ())),
                    preferred_element_type=F32,
                )
                scores = scores + bias
                top = jnp.max(scores, axis=-1, keepdims=True)
                weights = jnp.exp(scores - top).astype(BF16)
                parts.append(jnp.dot(weights, value_v[head], preferred_element_type=F32))
            summed = jnp.where(half, parts[0], parts[1])
            total = pltpu.roll(jnp.where(half, parts[1], parts[0]), 64, 1)
            att_v[rows, pair * 128 : pair * 128 + 128] = (summed / total).astype(BF16)
        for peer in range(4):
            home = layer * 4 + peer

            @pl.when(home != me)
            def _(home=home):
                give(home).start()

            @pl.when(home == me)
            def _(home=home):
                pltpu.make_async_copy(
                    att_v.at[pl.ds(pl.multiple_of(home * ROWS, ROWS), ROWS), :],
                    back_v.at[z, :, home_cols],
                    local_sem.at[9],
                ).start()

        return carry

    lax.fori_loop(0, LAYERS, attend, 0)

    def home_recv(d, carry):
        peer = lax.rem(me + d, GROUP)
        remote(
            att_v.at[pl.ds(0, ROWS), :],
            back_v.at[peer // 4, :, pl.ds(pl.multiple_of(lax.rem(peer, 4) * COLS, COLS), COLS)],
            ret_send.at[peer],
            ret_recv.at[peer],
            tm,
            peer,
        ).wait_recv()
        return carry

    pltpu.make_async_copy(
        att_v.at[pl.ds(0, ROWS), :], back_v.at[z, :, home_cols], local_sem.at[9]
    ).wait()
    lax.fori_loop(1, GROUP, home_recv, 0)
    loads[6].wait()
    projected = jnp.dot(
        back_v[...].reshape(4 * ROWS, WIDTH), wo_v[...], preferred_element_type=F32
    )
    result[...] = (
        (second_v[...].astype(F32) + projected).astype(BF16).reshape(4, ROWS, WIDTH)
    )

    @pl.when(tm < n_tm - 1)
    def _():
        for step in order:
            shift(step).wait_send()

    def drained(d, carry):
        peer = lax.rem(me + d, GROUP)
        info_copy(me, peer).wait_send()
        give(peer).wait_send()
        return carry

    lax.fori_loop(1, GROUP, drained, 0)
    for step in range(4):
        sent = remote(
            mine_v.at[step], gath_v.at[me], ex_send.at[step * 2 + 1], ex_recv.at[me], tm, across
        )
        sent.wait_send()
        sent = remote(
            mine_v.at[step], gath_v.at[me], ex_send.at[step * 2], ex_recv.at[me], tm, across
        )

        @pl.when(z != step)
        def _(sent=sent):
            sent.wait_send()

    for turn in turns:
        for slot in slots(turn):
            forward(slot).wait_send()


def per_device(
    tokens,
    conv_taps,
    norm_first,
    norm_second,
    norm_third,
    w_in,
    w_out,
    w_query,
    w_key,
    w_value,
    w_output,
    agent_order,
    present_steps,
):
    places = jnp.concatenate([agent_order, agent_order])
    untils = jnp.concatenate([present_steps, present_steps])
    info = jnp.stack([places, untils] * 4)
    vmem, hbm = pl.BlockSpec(memory_space=pltpu.VMEM), pl.BlockSpec(memory_space=pl.ANY)
    dma = pltpu.SemaphoreType.DMA
    everyone = GROUP * ROWS
    return pl.pallas_call(
        block_kernel,
        out_shape=jax.ShapeDtypeStruct(tokens.shape, BF16),
        in_specs=[hbm] + [vmem] * 4 + [hbm] * 6 + [vmem],
        out_specs=vmem,
        scratch_shapes=[
            pltpu.VMEM((WIDTH, HIDDEN), BF16),
            pltpu.VMEM((HIDDEN, WIDTH), BF16),
            pltpu.VMEM((3, WIDTH, COLS), BF16),
            pltpu.VMEM((WIDTH, WIDTH), BF16),
            pltpu.VMEM((4, ROWS, WIDTH), BF16),
            pltpu.VMEM((4, ROWS, WIDTH), BF16),
            pltpu.VMEM((8, ROWS, WIDTH), F32),
            pltpu.VMEM((4 * ROWS, HIDDEN), BF16),
            pltpu.VMEM((4 * ROWS, WIDTH), BF16),
            pltpu.VMEM((4, ROWS, WIDTH), BF16),
            pltpu.VMEM((GROUP, ROWS, WIDTH), BF16),
            pltpu.VMEM((2, everyone, 128), BF16),
            pltpu.VMEM((4, everyone, 128), BF16),
            pltpu.VMEM((4, everyone, 128), BF16),
            pltpu.VMEM((everyone, COLS), BF16),
            pltpu.VMEM((4, ROWS, WIDTH), BF16),
            pltpu.VMEM((GROUP, 8, 128), jnp.int32),
            pltpu.VMEM((8, everyone), F32),
            pltpu.VMEM((everyone, 1), F32),
            dma((10,)),
            dma((4,)),
            dma((4,)),
            dma((GROUP,)),
            dma((GROUP,)),
            dma((8,)),
            dma((GROUP,)),
            dma((GROUP,)),
            dma((GROUP,)),
            dma((GROUP,)),
            dma((GROUP,)),
        ],
        compiler_params=pltpu.CompilerParams(
            collective_id=0, has_side_effects=True, vmem_limit_bytes=60 << 20
        ),
        name="space_time_block",
    )(
        tokens,
        conv_taps,
        norm_first.reshape(1, WIDTH),
        norm_second.reshape(1, WIDTH),
        norm_third.reshape(1, WIDTH),
        w_in,
        w_out,
        w_query,
        w_key,
        w_value,
        w_output,
        info,
    )


def solution(mesh):
    rows = P("tm", "agent", None)
    whole = P()
    return jax.shard_map(
        per_device,
        mesh=mesh,
        in_specs=(rows,) + (whole,) * 10 + (P("agent"), P("agent")),
        out_specs=rows,
        check_vma=False,
    )
```

```python
import functools

import jax
import jax.numpy as jnp
from jax import lax
from jax.experimental import pallas as pl
from jax.experimental.pallas import tpu as pltpu
from jax.sharding import PartitionSpec as P

EPS = 1e-05
HEADS = 16
MESH = pl.DeviceIdType.MESH
F32, BF16 = jnp.float32, jnp.bfloat16
GROUP = 16
ROWS = 64
WIDTH = 1024
HIDDEN = 3072
COLS = 256
FF_TILE = 1024
PIECES = 2
PIECE = ROWS // PIECES
SPAN = GROUP * PIECE
QUERIES = 256
HOMES = QUERIES // PIECE
SENDS = ((0, 1), (1, 0), (3, 0), (1, 1), (3, 1), (2, 0), (2, 1))


def remote(src, dst, send, recv, tm, agent):
    return pltpu.make_async_remote_copy(
        src_ref=src,
        dst_ref=dst,
        send_sem=send,
        recv_sem=recv,
        device_id=(tm, agent),
        device_id_type=MESH,
    )


def normed(rows, gain):
    scale = lax.rsqrt(jnp.mean(rows * rows, axis=-1, keepdims=True) + EPS)
    return rows * scale * gain


def block_kernel(
    tokens,
    taps,
    gain_first,
    gain_second,
    gain_third,
    w_in,
    w_out,
    w_query,
    w_key,
    w_value,
    w_output,
    order_own,
    present_own,
    result,
    win_v,
    wout_v,
    wqkv_v,
    wo_v,
    tok_v,
    prev_v,
    norm_v,
    inner_v,
    hid_v,
    second_v,
    mine_v,
    gath_v,
    query_v,
    key_v,
    value_v,
    att_v,
    back_v,
    info_v,
    okey_v,
    oquery_v,
    keep_v,
    local_sem,
    keep_sem,
    here_sem,
    shift_send,
    shift_recv,
    info_send,
    info_recv,
    ex_send,
    ex_recv,
    rel_send,
    rel_recv,
    ret_send,
    ret_recv,
):
    tm, me = lax.axis_index("tm"), lax.axis_index("agent")
    n_tm = lax.axis_size("tm")
    z, x, core = me // 4, lax.rem(me // 2, 2), lax.rem(me, 2)
    group = lax.rem(me, 4)
    sibling = me + 1 - 2 * core
    after, before = lax.rem(tm + 1, n_tm), lax.rem(tm + n_tm - 1, n_tm)

    cols = pl.ds(pl.multiple_of(group * COLS, COLS), COLS)
    loads = [
        pltpu.make_async_copy(tokens, tok_v, local_sem.at[0]),
        pltpu.make_async_copy(w_in, win_v, local_sem.at[1]),
        pltpu.make_async_copy(w_out, wout_v, local_sem.at[2]),
        pltpu.make_async_copy(w_query.at[:, cols], wqkv_v.at[0], local_sem.at[3]),
        pltpu.make_async_copy(w_key.at[:, cols], wqkv_v.at[1], local_sem.at[4]),
        pltpu.make_async_copy(w_value.at[:, cols], wqkv_v.at[2], local_sem.at[5]),
        pltpu.make_async_copy(w_output, wo_v, local_sem.at[6]),
    ]
    for load in loads:
        load.start()

    barrier = pltpu.get_barrier_semaphore()

    def greet(d, carry):
        pl.semaphore_signal(
            barrier, inc=1, device_id=(tm, lax.rem(me + d, GROUP)), device_id_type=MESH
        )
        return carry

    pl.semaphore_signal(barrier, inc=1, device_id=(before, me), device_id_type=MESH)
    pl.semaphore_signal(barrier, inc=1, device_id=(after, me), device_id_type=MESH)
    lax.fori_loop(1, GROUP, greet, 0)

    band = lax.rem(lax.broadcasted_iota(jnp.int32, (1, 128), 1) // PIECE, PIECES)
    info_v[me] = jnp.zeros((8, 128), jnp.int32)
    for number, source in enumerate((order_own, present_own)):
        info_v[me, 0:1, 0:ROWS] = source[...]
        once = info_v[me, 0:1, :]
        row = once + pltpu.roll(once, ROWS, 1)
        turned = [row] + [pltpu.roll(row, PIECE * i, 1) for i in range(1, PIECES)]
        for piece in range(PIECES):
            picked = row
            for i in range(1, PIECES):
                picked = jnp.where(lax.rem(band + PIECES - i, PIECES) == piece, turned[i], picked)
            keep_v[number * PIECES + piece : number * PIECES + piece + 1, :] = picked
    info_v[me, 0 : 2 * PIECES, :] = keep_v[0 : 2 * PIECES, :]

    pl.semaphore_wait(barrier, GROUP + 1)

    def shift(piece):
        rows = pl.ds(pl.multiple_of(piece * PIECE, PIECE), PIECE)
        return remote(
            tokens.at[:, rows, :],
            prev_v.at[:, rows, :],
            shift_send.at[piece],
            shift_recv.at[piece],
            after,
            me,
        )

    def info_copy(slot, peer):
        return remote(
            info_v.at[me], info_v.at[slot], info_send.at[peer], info_recv.at[slot], tm, peer
        )

    def tell(d, carry):
        info_copy(me, lax.rem(me + d, GROUP)).start()
        return carry

    lax.fori_loop(1, GROUP, tell, 0)

    @pl.when(tm < n_tm - 1)
    def _():
        for piece in range(PIECES):
            shift(piece).start()

    @pl.when(tm == 0)
    def _():
        def clear(i, carry):
            prev_v[i // 4, pl.ds(pl.multiple_of(lax.rem(i, 4) * 16, 16), 16), :] = jnp.zeros(
                (16, WIDTH), BF16
            )
            return carry

        lax.fori_loop(0, ROWS // 4, clear, 0)

    gain1, gain2, gain3 = gain_first[...], gain_second[...], gain_third[...]
    loads[0].wait()

    def feed(piece):
        rows = pl.ds(pl.multiple_of(piece * PIECE, PIECE), PIECE)
        for step in range(4):
            norm_v[4 + step] = normed(tok_v[step, rows].astype(F32), gain1)

        @pl.when(tm > 0)
        def _():
            shift(piece).wait_recv()

        for step in range(4):
            norm_v[step] = normed(prev_v[step, rows].astype(F32), gain1)
        firsts = []
        for step in range(4):
            mixed = taps[0:1, :] * norm_v[step + 4]
            for lag in range(1, 5):
                mixed = mixed + taps[lag : lag + 1, :] * norm_v[step + 4 - lag]
            firsts.append((tok_v[step, rows].astype(F32) + mixed).astype(BF16))
        first = jnp.concatenate(firsts, axis=0)
        second_v[piece] = first
        inner = normed(first.astype(F32), gain2).astype(BF16)
        inner_v[...] = inner

        def hidden(tile, carry):
            across = pl.ds(pl.multiple_of(tile * FF_TILE, FF_TILE), FF_TILE)
            pre = jnp.dot(inner_v[...], win_v[:, across], preferred_element_type=F32)
            act = 0.5 * pre * (1.0 + lax.erf(pre * 0.7071067811865476))
            hid_v[:, across] = act.astype(BF16)
            return carry

        lax.fori_loop(0, HIDDEN // FF_TILE, hidden, 0)
        ffn = jnp.dot(hid_v[...], wout_v[...], preferred_element_type=F32)
        second = (second_v[piece].astype(F32) + ffn).astype(BF16)
        second_v[piece] = second
        attn_in = normed(second.astype(F32), gain3).astype(BF16)
        for step in range(4):
            mine_v[piece, step] = attn_in[step * PIECE : (step + 1) * PIECE]

    def to_step(piece, turn, other):
        spot = piece * 8 + turn * 2 + other
        step = lax.rem(z + turn, 4)
        return remote(
            mine_v.at[piece, step],
            gath_v.at[piece, me],
            ex_send.at[spot],
            ex_recv.at[piece * GROUP + me],
            tm,
            step * 4 + 2 * ((1 - x) if other else x) + core,
        )

    def keep(piece):
        return pltpu.make_async_copy(
            mine_v.at[piece, z], gath_v.at[piece, me], keep_sem.at[piece]
        )

    def own_to_sibling(piece):
        return remote(
            mine_v.at[piece, z],
            gath_v.at[piece, me],
            rel_send.at[piece * GROUP + me],
            rel_recv.at[piece * GROUP + me],
            tm,
            sibling,
        )

    def spread(piece):
        @pl.when(tm == 0)
        def _():
            shift(piece).wait_send()

        keep(piece).start()
        own_to_sibling(piece).start()
        for turn, other in SENDS:
            to_step(piece, turn, other).start()


    def forward(piece, slot):
        return remote(
            gath_v.at[piece, slot],
            gath_v.at[piece, slot],
            rel_send.at[piece * GROUP + slot],
            rel_recv.at[piece * GROUP + slot],
            tm,
            sibling,
        )

    def others():
        return [
            lax.rem(z + 4 - turn, 4) * 4 + 2 * ((1 - x) if other else x) + core
            for turn, other in SENDS
        ]

    def relay(piece):
        for slot in others():
            remote(
                mine_v.at[piece, 0],
                gath_v.at[piece, slot],
                ex_send.at[0],
                ex_recv.at[piece * GROUP + slot],
                tm,
                slot,
            ).wait_recv()
            forward(piece, slot).start()

    lane = lax.broadcasted_iota(jnp.int32, (SPAN, 128), 1) < 64

    def project(piece):
        for slot in others() + [me]:
            forward(piece, slot + 1 - 2 * core).wait_recv()
        keep(piece).wait()
        rows = pl.ds(pl.multiple_of(piece * SPAN, SPAN), SPAN)
        source = gath_v[piece].reshape(SPAN, WIDTH)
        query = jnp.dot(source, wqkv_v[0], preferred_element_type=F32) * 0.125
        key = jnp.dot(source, wqkv_v[1], preferred_element_type=F32)
        value = jnp.dot(source, wqkv_v[2], preferred_element_type=F32)
        for pair in range(2):
            span = slice(pair * 128, pair * 128 + 128)
            query_v[pair, rows, :] = query[:, span].astype(BF16)
            key_v[2 * pair, rows, :] = jnp.where(lane, key[:, span], 0.0).astype(BF16)
            key_v[2 * pair + 1, rows, :] = jnp.where(lane, 0.0, key[:, span]).astype(BF16)
            value_v[2 * pair, rows, :] = jnp.where(lane, value[:, span], 1.0).astype(BF16)
            value_v[2 * pair + 1, rows, :] = jnp.where(lane, 1.0, value[:, span]).astype(BF16)

    def places():
        def heard(d, carry):
            peer = lax.rem(me + d, GROUP)
            info_copy(peer, peer).wait_recv()
            return carry

        lax.fori_loop(1, GROUP, heard, 0)
        now = tm * 4 + z
        eye = lax.broadcasted_iota(jnp.int32, (128, 128), 0) == lax.broadcasted_iota(
            jnp.int32, (128, 128), 1
        )
        part = lax.broadcasted_iota(jnp.int32, (1, 128), 1) // PIECE
        several = 128 // PIECE
        for piece in range(PIECES):
            for bunch in range(GROUP // several):
                place = info_v[bunch * several, piece : piece + 1]
                until = info_v[bunch * several, PIECES + piece : PIECES + piece + 1]
                for i in range(1, several):
                    tile = bunch * several + i
                    place = jnp.where(part == i, info_v[tile, piece : piece + 1], place)
                    until = jnp.where(
                        part == i, info_v[tile, PIECES + piece : PIECES + piece + 1], until
                    )
                place_f = place.astype(F32)
                start = piece * SPAN + bunch * 128
                okey_v[0:1, start : start + 128] = jnp.where(now < until, place_f, 1e9)
                oquery_v[start : start + 128, :] = jnp.sum(
                    jnp.where(eye, jnp.broadcast_to(place_f, (128, 128)), 0.0),
                    axis=1,
                    keepdims=True,
                )

    places()
    for load in loads[1:6]:
        load.wait()

    def produce(piece, carry):
        feed(piece)
        spread(piece)
        return carry

    def consume(piece, carry):
        relay(piece)
        project(piece)
        return carry

    lax.fori_loop(0, PIECES, produce, 0)
    lax.fori_loop(0, PIECES, consume, 0)


    def give(piece, home):
        return (
            att_v.at[pl.ds(pl.multiple_of(piece * SPAN + home * PIECE, PIECE), PIECE), :],
            back_v.at[piece, group, z],
        )

    def give_far(piece, home):
        source, target = give(piece, home)
        return remote(
            source,
            target,
            ret_send.at[piece * GROUP + home],
            ret_recv.at[piece * GROUP + me],
            tm,
            home,
        )

    def give_here(piece):
        source, target = give(piece, me)
        return pltpu.make_async_copy(source, target, here_sem.at[piece])

    half = lax.broadcasted_iota(jnp.int32, (QUERIES, 128), 1) < 64

    def attend(index, carry):
        start = pl.multiple_of(index * QUERIES, QUERIES)
        rows = pl.ds(start, QUERIES)
        row = lax.broadcasted_iota(jnp.int32, (QUERIES, GROUP * ROWS), 0) + start
        column = lax.broadcasted_iota(jnp.int32, (QUERIES, GROUP * ROWS), 1)
        visible = (okey_v[0:1, :] < oquery_v[rows, :]) | (row == column)
        bias = jnp.where(visible, 0.0, -1e30)
        for pair in range(2):
            query = query_v[pair, rows, :]
            parts = []
            for head in (2 * pair, 2 * pair + 1):
                scores = lax.dot_general(
                    query,
                    key_v[head],
                    (((1,), (1,)), ((), ())),
                    preferred_element_type=F32,
                )
                scores = scores + bias
                top = jnp.max(scores, axis=-1, keepdims=True)
                weights = jnp.exp(scores - top).astype(BF16)
                parts.append(jnp.dot(weights, value_v[head], preferred_element_type=F32))
            summed = jnp.where(half, parts[0], parts[1])
            total = pltpu.roll(jnp.where(half, parts[1], parts[0]), 64, 1)
            att_v[rows, pair * 128 : pair * 128 + 128] = (summed / total).astype(BF16)
        piece = start // SPAN
        first_home = lax.rem(start, SPAN) // PIECE
        for peer in range(HOMES):
            home = first_home + lax.rem(me + peer + 1, HOMES)

            @pl.when(home != me)
            def _(home=home):
                give_far(piece, home).start()

            @pl.when(home == me)
            def _():
                give_here(piece).start()

        return carry

    lax.fori_loop(0, GROUP * ROWS // QUERIES, attend, 0)

    loads[6].wait()
    def gather_home(piece, carry):
        give_here(piece).wait()

        def home_recv(d, carry):
            peer = lax.rem(me + d, GROUP)
            remote(
                att_v.at[pl.ds(0, PIECE), :],
                back_v.at[piece, lax.rem(peer, 4), peer // 4],
                ret_send.at[piece * GROUP + peer],
                ret_recv.at[piece * GROUP + peer],
                tm,
                peer,
            ).wait_recv()
            return carry

        lax.fori_loop(1, GROUP, home_recv, 0)
        attended = jnp.concatenate(
            [back_v[piece, heads].reshape(4 * PIECE, COLS) for heads in range(4)], axis=1
        )
        projected = jnp.dot(attended, wo_v[...], preferred_element_type=F32)
        done = (second_v[piece].astype(F32) + projected).astype(BF16)
        for step in range(4):
            result[step, pl.ds(pl.multiple_of(piece * PIECE, PIECE), PIECE), :] = done[
                step * PIECE : (step + 1) * PIECE
            ]
        return carry

    lax.fori_loop(0, PIECES, gather_home, 0)

    @pl.when((tm > 0) & (tm < n_tm - 1))
    def _():
        for piece in range(PIECES):
            shift(piece).wait_send()

    def drained(d, carry):
        peer = lax.rem(me + d, GROUP)
        info_copy(me, peer).wait_send()
        for piece in range(PIECES):
            give_far(piece, peer).wait_send()
        return carry

    lax.fori_loop(1, GROUP, drained, 0)
    for piece in range(PIECES):
        for turn, other in SENDS:
            to_step(piece, turn, other).wait_send()
        for slot in others() + [me]:
            forward(piece, slot).wait_send()


def per_device(
    tokens,
    conv_taps,
    norm_first,
    norm_second,
    norm_third,
    w_in,
    w_out,
    w_query,
    w_key,
    w_value,
    w_output,
    agent_order,
    present_steps,
):
    vmem, hbm = pl.BlockSpec(memory_space=pltpu.VMEM), pl.BlockSpec(memory_space=pl.ANY)
    dma = pltpu.SemaphoreType.DMA
    everyone = GROUP * ROWS
    return pl.pallas_call(
        block_kernel,
        out_shape=pltpu.VMEM(tokens.shape, BF16),
        in_specs=[hbm] + [vmem] * 4 + [hbm] * 6 + [vmem] * 2,
        out_specs=vmem,
        scratch_shapes=[
            pltpu.VMEM((WIDTH, HIDDEN), BF16),
            pltpu.VMEM((HIDDEN, WIDTH), BF16),
            pltpu.VMEM((3, WIDTH, COLS), BF16),
            pltpu.VMEM((WIDTH, WIDTH), BF16),
            pltpu.VMEM((4, ROWS, WIDTH), BF16),
            pltpu.VMEM((4, ROWS, WIDTH), BF16),
            pltpu.VMEM((8, PIECE, WIDTH), F32),
            pltpu.VMEM((4 * PIECE, WIDTH), BF16),
            pltpu.VMEM((4 * PIECE, HIDDEN), BF16),
            pltpu.VMEM((PIECES, 4 * PIECE, WIDTH), BF16),
            pltpu.VMEM((PIECES, 4, PIECE, WIDTH), BF16),
            pltpu.VMEM((PIECES, GROUP, PIECE, WIDTH), BF16),
            pltpu.VMEM((2, everyone, 128), BF16),
            pltpu.VMEM((4, everyone, 128), BF16),
            pltpu.VMEM((4, everyone, 128), BF16),
            pltpu.VMEM((everyone, COLS), BF16),
            pltpu.VMEM((PIECES, 4, 4, PIECE, COLS), BF16),
            pltpu.VMEM((GROUP, 8, 128), jnp.int32),
            pltpu.VMEM((8, everyone), F32),
            pltpu.VMEM((everyone, 1), F32),
            pltpu.VMEM((8, 128), jnp.int32),
            dma((7,)),
            dma((PIECES,)),
            dma((PIECES,)),
            dma((PIECES,)),
            dma((PIECES,)),
            dma((GROUP,)),
            dma((GROUP,)),
            dma((PIECES * 8,)),
            dma((PIECES * GROUP,)),
            dma((PIECES * GROUP,)),
            dma((PIECES * GROUP,)),
            dma((PIECES * GROUP,)),
            dma((PIECES * GROUP,)),
        ],
        compiler_params=pltpu.CompilerParams(
            collective_id=0, has_side_effects=True, vmem_limit_bytes=60 << 20
        ),
        name="space_time_block",
    )(
        tokens,
        conv_taps,
        norm_first.reshape(1, WIDTH),
        norm_second.reshape(1, WIDTH),
        norm_third.reshape(1, WIDTH),
        w_in,
        w_out,
        w_query,
        w_key,
        w_value,
        w_output,
        agent_order.reshape(1, ROWS),
        present_steps.reshape(1, ROWS),
    )


def solution(mesh):
    rows = P("tm", "agent", None)
    whole = P()
    return jax.shard_map(
        per_device,
        mesh=mesh,
        in_specs=(rows,) + (whole,) * 10 + (P("agent"), P("agent")),
        out_specs=rows,
        check_vma=False,
    )
```

```python
import functools

import jax
import jax.numpy as jnp
from jax import lax
from jax.experimental import pallas as pl
from jax.experimental.pallas import tpu as pltpu
from jax.sharding import PartitionSpec as P

EPS = 1e-05
HEADS = 16
MESH = pl.DeviceIdType.MESH
F32, BF16 = jnp.float32, jnp.bfloat16
GROUP = 16
ROWS = 64
WIDTH = 1024
HIDDEN = 3072
COLS = 256
FF_TILE = 1024
PIECES = 2
PIECE = ROWS // PIECES
SPAN = GROUP * PIECE
QUERIES = 256
HOMES = QUERIES // PIECE
SENDS = ((0, 1), (1, 0), (3, 0), (1, 1), (3, 1), (2, 0), (2, 1))


def remote(src, dst, send, recv, tm, agent):
    return pltpu.make_async_remote_copy(
        src_ref=src,
        dst_ref=dst,
        send_sem=send,
        recv_sem=recv,
        device_id=(tm, agent),
        device_id_type=MESH,
    )


def normed(rows, gain):
    scale = lax.rsqrt(jnp.mean(rows * rows, axis=-1, keepdims=True) + EPS)
    return rows * scale * gain


def block_kernel(
    tokens,
    taps,
    gain_first,
    gain_second,
    gain_third,
    w_in,
    w_out,
    w_query,
    w_key,
    w_value,
    w_output,
    order_own,
    present_own,
    result,
    win_v,
    wout_v,
    wqkv_v,
    wo_v,
    tok_v,
    prev_v,
    norm_v,
    inner_v,
    hid_v,
    second_v,
    mine_v,
    gath_v,
    query_v,
    key_v,
    value_v,
    att_v,
    back_v,
    info_v,
    okey_v,
    oquery_v,
    keep_v,
    top_v,
    part_v,
    local_sem,
    keep_sem,
    here_sem,
    shift_send,
    shift_recv,
    info_send,
    info_recv,
    ex_send,
    ex_recv,
    rel_send,
    rel_recv,
    ret_send,
    ret_recv,
):
    tm, me = lax.axis_index("tm"), lax.axis_index("agent")
    n_tm = lax.axis_size("tm")
    z, x, core = me // 4, lax.rem(me // 2, 2), lax.rem(me, 2)
    group = lax.rem(me, 4)
    sibling = me + 1 - 2 * core
    after, before = lax.rem(tm + 1, n_tm), lax.rem(tm + n_tm - 1, n_tm)

    cols = pl.ds(pl.multiple_of(group * COLS, COLS), COLS)
    loads = [
        pltpu.make_async_copy(tokens, tok_v, local_sem.at[0]),
        pltpu.make_async_copy(w_in, win_v, local_sem.at[1]),
        pltpu.make_async_copy(w_out, wout_v, local_sem.at[2]),
        pltpu.make_async_copy(w_query.at[:, cols], wqkv_v.at[0], local_sem.at[3]),
        pltpu.make_async_copy(w_key.at[:, cols], wqkv_v.at[1], local_sem.at[4]),
        pltpu.make_async_copy(w_value.at[:, cols], wqkv_v.at[2], local_sem.at[5]),
        pltpu.make_async_copy(w_output, wo_v, local_sem.at[6]),
    ]
    for load in loads:
        load.start()

    barrier = pltpu.get_barrier_semaphore()

    def greet(d, carry):
        pl.semaphore_signal(
            barrier, inc=1, device_id=(tm, lax.rem(me + d, GROUP)), device_id_type=MESH
        )
        return carry

    @pl.when(tm > 0)
    def _():
        pl.semaphore_signal(barrier, inc=1, device_id=(before, me), device_id_type=MESH)

    lax.fori_loop(1, GROUP, greet, 0)

    band = lax.rem(lax.broadcasted_iota(jnp.int32, (1, 128), 1) // PIECE, PIECES)
    info_v[me] = jnp.zeros((8, 128), jnp.int32)
    for number, source in enumerate((order_own, present_own)):
        info_v[me, 0:1, 0:ROWS] = source[...]
        once = info_v[me, 0:1, :]
        row = once + pltpu.roll(once, ROWS, 1)
        turned = [row] + [pltpu.roll(row, PIECE * i, 1) for i in range(1, PIECES)]
        for piece in range(PIECES):
            picked = row
            for i in range(1, PIECES):
                picked = jnp.where(lax.rem(band + PIECES - i, PIECES) == piece, turned[i], picked)
            keep_v[number * PIECES + piece : number * PIECES + piece + 1, :] = picked
    info_v[me, 0 : 2 * PIECES, :] = keep_v[0 : 2 * PIECES, :]

    @pl.when(tm < n_tm - 1)
    def _():
        pl.semaphore_wait(barrier, GROUP)

    @pl.when(tm == n_tm - 1)
    def _():
        pl.semaphore_wait(barrier, GROUP - 1)


    def shift(piece):
        rows = pl.ds(pl.multiple_of(piece * PIECE, PIECE), PIECE)
        return remote(
            tokens.at[:, rows, :],
            prev_v.at[:, rows, :],
            shift_send.at[piece],
            shift_recv.at[piece],
            after,
            me,
        )

    def info_copy(slot, peer):
        return remote(
            info_v.at[me], info_v.at[slot], info_send.at[peer], info_recv.at[slot], tm, peer
        )

    def tell(d, carry):
        info_copy(me, lax.rem(me + d, GROUP)).start()
        return carry

    lax.fori_loop(1, GROUP, tell, 0)

    @pl.when(tm < n_tm - 1)
    def _():
        for piece in range(PIECES):
            shift(piece).start()

    @pl.when(tm == 0)
    def _():
        def clear(i, carry):
            prev_v[i // 4, pl.ds(pl.multiple_of(lax.rem(i, 4) * 16, 16), 16), :] = jnp.zeros(
                (16, WIDTH), BF16
            )
            return carry

        lax.fori_loop(0, ROWS // 4, clear, 0)

    gain1, gain2, gain3 = gain_first[...], gain_second[...], gain_third[...]
    loads[0].wait()

    def feed(piece):
        rows = pl.ds(pl.multiple_of(piece * PIECE, PIECE), PIECE)
        for step in range(4):
            norm_v[4 + step] = normed(tok_v[step, rows].astype(F32), gain1)

        @pl.when(tm > 0)
        def _():
            shift(piece).wait_recv()

        for step in range(4):
            norm_v[step] = normed(prev_v[step, rows].astype(F32), gain1)
        firsts = []
        for step in range(4):
            mixed = taps[0:1, :] * norm_v[step + 4]
            for lag in range(1, 5):
                mixed = mixed + taps[lag : lag + 1, :] * norm_v[step + 4 - lag]
            firsts.append((tok_v[step, rows].astype(F32) + mixed).astype(BF16))
        first = jnp.concatenate(firsts, axis=0)
        second_v[piece] = first
        inner = normed(first.astype(F32), gain2).astype(BF16)
        inner_v[...] = inner

        def hidden(tile, carry):
            across = pl.ds(pl.multiple_of(tile * FF_TILE, FF_TILE), FF_TILE)
            pre = jnp.dot(inner_v[...], win_v[:, across], preferred_element_type=F32)
            act = 0.5 * pre * (1.0 + lax.erf(pre * 0.7071067811865476))
            hid_v[:, across] = act.astype(BF16)
            return carry

        lax.fori_loop(0, HIDDEN // FF_TILE, hidden, 0)
        ffn = jnp.dot(hid_v[...], wout_v[...], preferred_element_type=F32)
        second = (second_v[piece].astype(F32) + ffn).astype(BF16)
        second_v[piece] = second
        attn_in = normed(second.astype(F32), gain3).astype(BF16)
        for step in range(4):
            mine_v[piece, step] = attn_in[step * PIECE : (step + 1) * PIECE]

    def to_step(piece, turn, other):
        spot = piece * 8 + turn * 2 + other
        step = lax.rem(z + turn, 4)
        return remote(
            mine_v.at[piece, step],
            gath_v.at[piece, me],
            ex_send.at[spot],
            ex_recv.at[piece * GROUP + me],
            tm,
            step * 4 + 2 * ((1 - x) if other else x) + core,
        )

    def keep(piece):
        return pltpu.make_async_copy(
            mine_v.at[piece, z], gath_v.at[piece, me], keep_sem.at[piece]
        )

    def own_to_sibling(piece):
        return remote(
            mine_v.at[piece, z],
            gath_v.at[piece, me],
            rel_send.at[piece * GROUP + me],
            rel_recv.at[piece * GROUP + me],
            tm,
            sibling,
        )

    def spread(piece):
        @pl.when(tm == 0)
        def _():
            shift(piece).wait_send()

        keep(piece).start()
        own_to_sibling(piece).start()
        for turn, other in SENDS:
            to_step(piece, turn, other).start()


    def forward(piece, slot):
        return remote(
            gath_v.at[piece, slot],
            gath_v.at[piece, slot],
            rel_send.at[piece * GROUP + slot],
            rel_recv.at[piece * GROUP + slot],
            tm,
            sibling,
        )

    def others():
        return [
            lax.rem(z + 4 - turn, 4) * 4 + 2 * ((1 - x) if other else x) + core
            for turn, other in SENDS
        ]

    def relay(piece):
        for slot in others():
            remote(
                mine_v.at[piece, 0],
                gath_v.at[piece, slot],
                ex_send.at[0],
                ex_recv.at[piece * GROUP + slot],
                tm,
                slot,
            ).wait_recv()
            forward(piece, slot).start()

    lane = lax.broadcasted_iota(jnp.int32, (SPAN, 128), 1) < 64

    def project(piece):
        for slot in others() + [me]:
            forward(piece, slot + 1 - 2 * core).wait_recv()
        keep(piece).wait()
        rows = pl.ds(pl.multiple_of(piece * SPAN, SPAN), SPAN)
        source = gath_v[piece].reshape(SPAN, WIDTH)
        query = jnp.dot(source, wqkv_v[0], preferred_element_type=F32) * 0.125
        key = jnp.dot(source, wqkv_v[1], preferred_element_type=F32)
        value = jnp.dot(source, wqkv_v[2], preferred_element_type=F32)
        for pair in range(2):
            span = slice(pair * 128, pair * 128 + 128)
            query_v[pair, rows, :] = query[:, span].astype(BF16)
            key_v[2 * pair, rows, :] = jnp.where(lane, key[:, span], 0.0).astype(BF16)
            key_v[2 * pair + 1, rows, :] = jnp.where(lane, 0.0, key[:, span]).astype(BF16)
            value_v[2 * pair, rows, :] = jnp.where(lane, value[:, span], 1.0).astype(BF16)
            value_v[2 * pair + 1, rows, :] = jnp.where(lane, 1.0, value[:, span]).astype(BF16)

    def places():
        def heard(d, carry):
            peer = lax.rem(me + d, GROUP)
            info_copy(peer, peer).wait_recv()
            return carry

        lax.fori_loop(1, GROUP, heard, 0)
        now = tm * 4 + z
        eye = lax.broadcasted_iota(jnp.int32, (128, 128), 0) == lax.broadcasted_iota(
            jnp.int32, (128, 128), 1
        )
        part = lax.broadcasted_iota(jnp.int32, (1, 128), 1) // PIECE
        several = 128 // PIECE
        for piece in range(PIECES):
            for bunch in range(GROUP // several):
                place = info_v[bunch * several, piece : piece + 1]
                until = info_v[bunch * several, PIECES + piece : PIECES + piece + 1]
                for i in range(1, several):
                    tile = bunch * several + i
                    place = jnp.where(part == i, info_v[tile, piece : piece + 1], place)
                    until = jnp.where(
                        part == i, info_v[tile, PIECES + piece : PIECES + piece + 1], until
                    )
                place_f = place.astype(F32)
                start = piece * SPAN + bunch * 128
                okey_v[0:1, start : start + 128] = jnp.where(now < until, place_f, 1e9)
                oquery_v[start : start + 128, :] = jnp.sum(
                    jnp.where(eye, jnp.broadcast_to(place_f, (128, 128)), 0.0),
                    axis=1,
                    keepdims=True,
                )

    places()
    for load in loads[1:6]:
        load.wait()

    def produce(piece, carry):
        feed(piece)
        spread(piece)
        return carry

    lax.fori_loop(0, PIECES, produce, 0)


    def give(piece, home):
        return (
            att_v.at[pl.ds(pl.multiple_of(piece * SPAN + home * PIECE, PIECE), PIECE), :],
            back_v.at[piece, group, z],
        )

    def give_far(piece, home):
        source, target = give(piece, home)
        return remote(
            source,
            target,
            ret_send.at[piece * GROUP + home],
            ret_recv.at[piece * GROUP + me],
            tm,
            home,
        )

    def give_here(piece):
        source, target = give(piece, me)
        return pltpu.make_async_copy(source, target, here_sem.at[piece])

    def heads(start, count, keys, combine):
        rows = pl.ds(start, count)
        width = keys.stop - keys.start
        row = lax.broadcasted_iota(jnp.int32, (count, width), 0) + start
        column = lax.broadcasted_iota(jnp.int32, (count, width), 1) + keys.start
        visible = (okey_v[0:1, keys] < oquery_v[rows, :]) | (row == column)
        bias = jnp.where(visible, 0.0, -1e30)

        def score(head):
            return lax.dot_general(
                query_v[head // 2, rows, :],
                key_v[head, keys, :],
                (((1,), (1,)), ((), ())),
                preferred_element_type=F32,
            )

        def weigh(head, scores):
            scores = scores + bias
            top = jnp.max(scores, axis=-1, keepdims=True)
            if combine:
                top = jnp.maximum(top, top_v[head, rows, :])
            return top, jnp.exp(scores - top).astype(BF16)

        def total(head, top, weights):
            part = jnp.dot(weights, value_v[head, keys, :], preferred_element_type=F32)
            if combine:
                part = part + part_v[head, rows, :] * jnp.exp(top_v[head, rows, :] - top)
            return part

        tops, parts = [], []
        ahead = score(0)
        behind = None
        for head in range(4):
            scores = ahead
            if head < 3:
                ahead = score(head + 1)
            top, weights = weigh(head, scores)
            if behind is not None:
                parts.append(total(head - 1, *behind))
            behind = (top, weights)
            tops.append(top)
        parts.append(total(3, *behind))
        return tops, parts

    def store(start, count, parts):
        half = lax.broadcasted_iota(jnp.int32, (count, 128), 1) < 64
        for pair in range(2):
            even, odd = parts[2 * pair : 2 * pair + 2]
            summed = jnp.where(half, even, odd)
            over = pltpu.roll(jnp.where(half, odd, even), 64, 1)
            att_v[pl.ds(start, count), pair * 128 : pair * 128 + 128] = (summed / over).astype(BF16)

    def send_home(piece, first_home, count):
        def one(peer, carry):
            home = first_home + lax.rem(me + peer + 1, count)

            @pl.when(home != me)
            def _():
                give_far(piece, home).start()

            @pl.when(home == me)
            def _():
                give_here(piece).start()

            return carry

        lax.fori_loop(0, count, one, 0)

    relay(0)
    project(0)

    def early(index, carry):
        start = pl.multiple_of(index * QUERIES, QUERIES)
        tops, parts = heads(start, QUERIES, slice(0, SPAN), False)
        for head in range(4):
            top_v[head, pl.ds(start, QUERIES), :] = tops[head]
            part_v[head, pl.ds(start, QUERIES), :] = parts[head]
        return carry

    lax.fori_loop(0, SPAN // QUERIES, early, 0)
    relay(1)
    project(1)

    def late(index, carry):
        start = pl.multiple_of(index * QUERIES, QUERIES)
        tops, parts = heads(start, QUERIES, slice(SPAN, 2 * SPAN), True)
        store(start, QUERIES, parts)
        send_home(0, index * HOMES, HOMES)
        return carry

    lax.fori_loop(0, SPAN // QUERIES, late, 0)

    def attend(index, carry):
        start = pl.multiple_of(SPAN + index * QUERIES, QUERIES)
        tops, parts = heads(start, QUERIES, slice(0, 2 * SPAN), False)
        store(start, QUERIES, parts)
        send_home(1, index * HOMES, HOMES)
        return carry

    lax.fori_loop(0, SPAN // QUERIES, attend, 0)

    loads[6].wait()
    def gather_home(piece, carry):
        give_here(piece).wait()

        def home_recv(d, carry):
            peer = lax.rem(me + d, GROUP)
            remote(
                att_v.at[pl.ds(0, PIECE), :],
                back_v.at[piece, lax.rem(peer, 4), peer // 4],
                ret_send.at[piece * GROUP + peer],
                ret_recv.at[piece * GROUP + peer],
                tm,
                peer,
            ).wait_recv()
            return carry

        lax.fori_loop(1, GROUP, home_recv, 0)
        attended = jnp.concatenate(
            [back_v[piece, quarter].reshape(4 * PIECE, COLS) for quarter in range(4)], axis=1
        )
        projected = jnp.dot(attended, wo_v[...], preferred_element_type=F32)
        done = (second_v[piece].astype(F32) + projected).astype(BF16)
        for step in range(4):
            result[step, pl.ds(pl.multiple_of(piece * PIECE, PIECE), PIECE), :] = done[
                step * PIECE : (step + 1) * PIECE
            ]
        return carry

    lax.fori_loop(0, PIECES, gather_home, 0)

    @pl.when((tm > 0) & (tm < n_tm - 1))
    def _():
        for piece in range(PIECES):
            shift(piece).wait_send()

    def drained(d, carry):
        peer = lax.rem(me + d, GROUP)
        info_copy(me, peer).wait_send()
        for piece in range(PIECES):
            give_far(piece, peer).wait_send()
        return carry

    lax.fori_loop(1, GROUP, drained, 0)
    for piece in range(PIECES):
        for turn, other in SENDS:
            to_step(piece, turn, other).wait_send()
        for slot in others() + [me]:
            forward(piece, slot).wait_send()


def per_device(
    tokens,
    conv_taps,
    norm_first,
    norm_second,
    norm_third,
    w_in,
    w_out,
    w_query,
    w_key,
    w_value,
    w_output,
    agent_order,
    present_steps,
):
    vmem, hbm = pl.BlockSpec(memory_space=pltpu.VMEM), pl.BlockSpec(memory_space=pl.ANY)
    dma = pltpu.SemaphoreType.DMA
    everyone = GROUP * ROWS
    return pl.pallas_call(
        block_kernel,
        out_shape=pltpu.VMEM(tokens.shape, BF16),
        in_specs=[hbm] + [vmem] * 4 + [hbm] * 6 + [vmem] * 2,
        out_specs=vmem,
        scratch_shapes=[
            pltpu.VMEM((WIDTH, HIDDEN), BF16),
            pltpu.VMEM((HIDDEN, WIDTH), BF16),
            pltpu.VMEM((3, WIDTH, COLS), BF16),
            pltpu.VMEM((WIDTH, WIDTH), BF16),
            pltpu.VMEM((4, ROWS, WIDTH), BF16),
            pltpu.VMEM((4, ROWS, WIDTH), BF16),
            pltpu.VMEM((8, PIECE, WIDTH), F32),
            pltpu.VMEM((4 * PIECE, WIDTH), BF16),
            pltpu.VMEM((4 * PIECE, HIDDEN), BF16),
            pltpu.VMEM((PIECES, 4 * PIECE, WIDTH), BF16),
            pltpu.VMEM((PIECES, 4, PIECE, WIDTH), BF16),
            pltpu.VMEM((PIECES, GROUP, PIECE, WIDTH), BF16),
            pltpu.VMEM((2, everyone, 128), BF16),
            pltpu.VMEM((4, everyone, 128), BF16),
            pltpu.VMEM((4, everyone, 128), BF16),
            pltpu.VMEM((everyone, COLS), BF16),
            pltpu.VMEM((PIECES, 4, 4, PIECE, COLS), BF16),
            pltpu.VMEM((GROUP, 8, 128), jnp.int32),
            pltpu.VMEM((8, everyone), F32),
            pltpu.VMEM((everyone, 1), F32),
            pltpu.VMEM((8, 128), jnp.int32),
            pltpu.VMEM((4, SPAN, 1), F32),
            pltpu.VMEM((4, SPAN, 128), F32),
            dma((7,)),
            dma((PIECES,)),
            dma((PIECES,)),
            dma((PIECES,)),
            dma((PIECES,)),
            dma((GROUP,)),
            dma((GROUP,)),
            dma((PIECES * 8,)),
            dma((PIECES * GROUP,)),
            dma((PIECES * GROUP,)),
            dma((PIECES * GROUP,)),
            dma((PIECES * GROUP,)),
            dma((PIECES * GROUP,)),
        ],
        compiler_params=pltpu.CompilerParams(
            collective_id=0, has_side_effects=True, vmem_limit_bytes=60 << 20
        ),
        name="space_time_block",
    )(
        tokens,
        conv_taps,
        norm_first.reshape(1, WIDTH),
        norm_second.reshape(1, WIDTH),
        norm_third.reshape(1, WIDTH),
        w_in,
        w_out,
        w_query,
        w_key,
        w_value,
        w_output,
        agent_order.reshape(1, ROWS),
        present_steps.reshape(1, ROWS),
    )


def solution(mesh):
    rows = P("tm", "agent", None)
    whole = P()
    return jax.shard_map(
        per_device,
        mesh=mesh,
        in_specs=(rows,) + (whole,) * 10 + (P("agent"), P("agent")),
        out_specs=rows,
        check_vma=False,
    )
```

```python
import functools

import jax
import jax.numpy as jnp
from jax import lax
from jax.experimental import pallas as pl
from jax.experimental.pallas import tpu as pltpu
from jax.sharding import PartitionSpec as P

EPS = 1e-05
HEADS = 16
MESH = pl.DeviceIdType.MESH
F32, BF16 = jnp.float32, jnp.bfloat16
GROUP = 16
ROWS = 64
WIDTH = 1024
HIDDEN = 3072
COLS = 256
FF_TILE = 1024
PIECES = 2
PIECE = ROWS // PIECES
SPAN = GROUP * PIECE
QUERIES = 256
HOMES = QUERIES // PIECE
SENDS = ((0, 1), (1, 0), (3, 0), (1, 1), (3, 1), (2, 0), (2, 1))


def remote(src, dst, send, recv, tm, agent):
    return pltpu.make_async_remote_copy(
        src_ref=src,
        dst_ref=dst,
        send_sem=send,
        recv_sem=recv,
        device_id=(tm, agent),
        device_id_type=MESH,
    )


def normed(rows, gain):
    scale = lax.rsqrt(jnp.mean(rows * rows, axis=-1, keepdims=True) + EPS)
    return rows * scale * gain


def block_kernel(
    tokens,
    taps_in,
    gain_first,
    gain_second,
    gain_third,
    w_in,
    w_out,
    w_query,
    w_key,
    w_value,
    w_output,
    order_own,
    present_own,
    result,
    taps,
    gains_v,
    own_v,
    win_v,
    wout_v,
    wqkv_v,
    wo_v,
    tok_v,
    prev_v,
    norm_v,
    inner_v,
    hid_v,
    second_v,
    mine_v,
    gath_v,
    query_v,
    key_v,
    value_v,
    att_v,
    back_v,
    info_v,
    okey_v,
    oquery_v,
    keep_v,
    top_v,
    part_v,
    small_sem,
    local_sem,
    keep_sem,
    here_sem,
    shift_send,
    shift_recv,
    info_send,
    info_recv,
    ex_send,
    ex_recv,
    rel_send,
    rel_recv,
    ret_send,
    ret_recv,
):
    tm, me = lax.axis_index("tm"), lax.axis_index("agent")
    n_tm = lax.axis_size("tm")
    z, x, core = me // 4, lax.rem(me // 2, 2), lax.rem(me, 2)
    group = lax.rem(me, 4)
    sibling = me + 1 - 2 * core
    after, before = lax.rem(tm + 1, n_tm), lax.rem(tm + n_tm - 1, n_tm)

    cols = pl.ds(pl.multiple_of(group * COLS, COLS), COLS)
    small = [
        pltpu.make_async_copy(taps_in, taps, small_sem.at[0]),
        pltpu.make_async_copy(gain_first, gains_v.at[0:1], small_sem.at[1]),
        pltpu.make_async_copy(gain_second, gains_v.at[1:2], small_sem.at[2]),
        pltpu.make_async_copy(gain_third, gains_v.at[2:3], small_sem.at[3]),
    ]
    loads = [
        pltpu.make_async_copy(tokens, tok_v, local_sem.at[0]),
        pltpu.make_async_copy(w_in, win_v, local_sem.at[1]),
        pltpu.make_async_copy(w_out, wout_v, local_sem.at[2]),
        pltpu.make_async_copy(w_query.at[:, cols], wqkv_v.at[0], local_sem.at[3]),
        pltpu.make_async_copy(w_key.at[:, cols], wqkv_v.at[1], local_sem.at[4]),
        pltpu.make_async_copy(w_value.at[:, cols], wqkv_v.at[2], local_sem.at[5]),
        pltpu.make_async_copy(w_output, wo_v, local_sem.at[6]),
    ]
    barrier = pltpu.get_barrier_semaphore()

    def greet(d, carry):
        pl.semaphore_signal(
            barrier, inc=1, device_id=(tm, lax.rem(me + d, GROUP)), device_id_type=MESH
        )
        return carry

    @pl.when(tm > 0)
    def _():
        pl.semaphore_signal(barrier, inc=1, device_id=(before, me), device_id_type=MESH)

    lax.fori_loop(1, GROUP, greet, 0)
    own_v[...] = jnp.zeros_like(own_v)
    for load in small + loads:
        load.start()
    own_v[0:1, 0:ROWS] = order_own[...]
    own_v[1:2, 0:ROWS] = present_own[...]

    band = lax.rem(lax.broadcasted_iota(jnp.int32, (1, 128), 1) // PIECE, PIECES)
    for number in range(2):
        once = own_v[number : number + 1, :]
        row = once + pltpu.roll(once, ROWS, 1)
        turned = [row] + [pltpu.roll(row, PIECE * i, 1) for i in range(1, PIECES)]
        for piece in range(PIECES):
            picked = row
            for i in range(1, PIECES):
                picked = jnp.where(lax.rem(band + PIECES - i, PIECES) == piece, turned[i], picked)
            keep_v[number * PIECES + piece : number * PIECES + piece + 1, :] = picked
    info_v[me] = keep_v[...]

    @pl.when(tm < n_tm - 1)
    def _():
        pl.semaphore_wait(barrier, GROUP)

    @pl.when(tm == n_tm - 1)
    def _():
        pl.semaphore_wait(barrier, GROUP - 1)


    def shift(piece):
        rows = pl.ds(pl.multiple_of(piece * PIECE, PIECE), PIECE)
        return remote(
            tokens.at[:, rows, :],
            prev_v.at[:, rows, :],
            shift_send.at[piece],
            shift_recv.at[piece],
            after,
            me,
        )

    def info_copy(slot, peer):
        return remote(
            info_v.at[me], info_v.at[slot], info_send.at[0], info_recv.at[0], tm, peer
        )

    def tell(d, carry):
        info_copy(me, lax.rem(me + d, GROUP)).start()
        return carry

    lax.fori_loop(1, GROUP, tell, 0)

    @pl.when(tm < n_tm - 1)
    def _():
        for piece in range(PIECES):
            shift(piece).start()

    @pl.when(tm == 0)
    def _():
        def clear(i, carry):
            prev_v[i // 4, pl.ds(pl.multiple_of(lax.rem(i, 4) * 16, 16), 16), :] = jnp.zeros(
                (16, WIDTH), BF16
            )
            return carry

        lax.fori_loop(0, ROWS // 4, clear, 0)

    for load in small:
        load.wait()
    gain1, gain2, gain3 = gains_v[0:1], gains_v[1:2], gains_v[2:3]
    loads[0].wait()

    def feed(piece):
        rows = pl.ds(pl.multiple_of(piece * PIECE, PIECE), PIECE)
        for step in range(4):
            norm_v[4 + step] = normed(tok_v[step, rows].astype(F32), gain1)

        @pl.when(tm > 0)
        def _():
            shift(piece).wait_recv()

        for step in range(4):
            norm_v[step] = normed(prev_v[step, rows].astype(F32), gain1)
        firsts = []
        for step in range(4):
            mixed = taps[0:1, :] * norm_v[step + 4]
            for lag in range(1, 5):
                mixed = mixed + taps[lag : lag + 1, :] * norm_v[step + 4 - lag]
            firsts.append((tok_v[step, rows].astype(F32) + mixed).astype(BF16))
        first = jnp.concatenate(firsts, axis=0)
        second_v[piece] = first
        inner = normed(first.astype(F32), gain2).astype(BF16)
        inner_v[...] = inner

        def hidden(tile, carry):
            across = pl.ds(pl.multiple_of(tile * FF_TILE, FF_TILE), FF_TILE)
            pre = jnp.dot(inner_v[...], win_v[:, across], preferred_element_type=F32)
            act = 0.5 * pre * (1.0 + lax.erf(pre * 0.7071067811865476))
            hid_v[:, across] = act.astype(BF16)
            return carry

        lax.fori_loop(0, HIDDEN // FF_TILE, hidden, 0)
        ffn = jnp.dot(hid_v[...], wout_v[...], preferred_element_type=F32)
        second = (second_v[piece].astype(F32) + ffn).astype(BF16)
        second_v[piece] = second
        attn_in = normed(second.astype(F32), gain3).astype(BF16)
        for step in range(4):
            mine_v[piece, step] = attn_in[step * PIECE : (step + 1) * PIECE]

    def to_step(piece, turn, other):
        step = lax.rem(z + turn, 4)
        return remote(
            mine_v.at[piece, step],
            gath_v.at[piece, me],
            ex_send.at[piece],
            ex_recv.at[piece * GROUP + me],
            tm,
            step * 4 + 2 * ((1 - x) if other else x) + core,
        )

    def keep(piece):
        return pltpu.make_async_copy(
            mine_v.at[piece, z], gath_v.at[piece, me], keep_sem.at[piece]
        )

    def own_to_sibling(piece):
        return remote(
            mine_v.at[piece, z],
            gath_v.at[piece, me],
            rel_send.at[piece],
            rel_recv.at[piece],
            tm,
            sibling,
        )

    def spread(piece):
        @pl.when(tm == 0)
        def _():
            shift(piece).wait_send()

        keep(piece).start()
        own_to_sibling(piece).start()
        for turn, other in SENDS:
            to_step(piece, turn, other).start()


    def forward(piece, slot):
        return remote(
            gath_v.at[piece, slot],
            gath_v.at[piece, slot],
            rel_send.at[piece],
            rel_recv.at[piece],
            tm,
            sibling,
        )

    def others():
        return [
            lax.rem(z + 4 - turn, 4) * 4 + 2 * ((1 - x) if other else x) + core
            for turn, other in SENDS
        ]

    def relay(piece):
        for slot in others():
            remote(
                mine_v.at[piece, 0],
                gath_v.at[piece, slot],
                ex_send.at[0],
                ex_recv.at[piece * GROUP + slot],
                tm,
                slot,
            ).wait_recv()
            forward(piece, slot).start()

    def relayed(piece):
        eight = gath_v.at[piece, pl.ds(0, GROUP // 2)]
        return remote(eight, eight, rel_send.at[piece], rel_recv.at[piece], tm, sibling)

    def spreaded(piece):
        seven = gath_v.at[piece, pl.ds(0, len(SENDS))]
        return remote(seven, seven, ex_send.at[piece], rel_recv.at[piece], tm, sibling)

    lane = lax.broadcasted_iota(jnp.int32, (SPAN, 128), 1) < 64

    def project(piece):
        relayed(piece).wait_recv()
        keep(piece).wait()
        rows = pl.ds(pl.multiple_of(piece * SPAN, SPAN), SPAN)
        source = gath_v[piece].reshape(SPAN, WIDTH)
        query = jnp.dot(source, wqkv_v[0], preferred_element_type=F32) * 0.125
        key = jnp.dot(source, wqkv_v[1], preferred_element_type=F32)
        value = jnp.dot(source, wqkv_v[2], preferred_element_type=F32)
        for pair in range(2):
            span = slice(pair * 128, pair * 128 + 128)
            query_v[pair, rows, :] = query[:, span].astype(BF16)
            key_v[2 * pair, rows, :] = jnp.where(lane, key[:, span], 0.0).astype(BF16)
            key_v[2 * pair + 1, rows, :] = jnp.where(lane, 0.0, key[:, span]).astype(BF16)
            value_v[2 * pair, rows, :] = jnp.where(lane, value[:, span], 1.0).astype(BF16)
            value_v[2 * pair + 1, rows, :] = jnp.where(lane, 1.0, value[:, span]).astype(BF16)

    def places():
        told = info_v.at[pl.ds(0, GROUP - 1)]
        both = remote(told, told, info_send.at[0], info_recv.at[0], tm, sibling)
        both.wait_recv()
        both.wait_send()
        now = tm * 4 + z
        eye = lax.broadcasted_iota(jnp.int32, (128, 128), 0) == lax.broadcasted_iota(
            jnp.int32, (128, 128), 1
        )
        part = lax.broadcasted_iota(jnp.int32, (1, 128), 1) // PIECE
        several = 128 // PIECE
        for piece in range(PIECES):
            for bunch in range(GROUP // several):
                place = info_v[bunch * several, piece : piece + 1]
                until = info_v[bunch * several, PIECES + piece : PIECES + piece + 1]
                for i in range(1, several):
                    tile = bunch * several + i
                    place = jnp.where(part == i, info_v[tile, piece : piece + 1], place)
                    until = jnp.where(
                        part == i, info_v[tile, PIECES + piece : PIECES + piece + 1], until
                    )
                place_f = place.astype(F32)
                start = piece * SPAN + bunch * 128
                okey_v[0:1, start : start + 128] = jnp.where(now < until, place_f, 1e9)
                oquery_v[start : start + 128, :] = jnp.sum(
                    jnp.where(eye, jnp.broadcast_to(place_f, (128, 128)), 0.0),
                    axis=1,
                    keepdims=True,
                )

    places()
    for load in loads[1:6]:
        load.wait()

    def produce(piece, carry):
        feed(piece)
        spread(piece)
        return carry

    lax.fori_loop(0, PIECES, produce, 0)


    def give(piece, home):
        return (
            att_v.at[pl.ds(pl.multiple_of(piece * SPAN + home * PIECE, PIECE), PIECE), :],
            back_v.at[piece, group, z],
        )

    def give_far(piece, home):
        source, target = give(piece, home)
        return remote(
            source,
            target,
            ret_send.at[piece],
            ret_recv.at[piece],
            tm,
            home,
        )

    def returned(piece):
        fifteen = att_v.at[pl.ds(0, (GROUP - 1) * PIECE), :]
        return remote(fifteen, fifteen, ret_send.at[piece], ret_recv.at[piece], tm, sibling)

    def give_here(piece):
        source, target = give(piece, me)
        return pltpu.make_async_copy(source, target, here_sem.at[piece])

    def heads(start, count, keys, combine):
        rows = pl.ds(start, count)
        width = keys.stop - keys.start
        row = lax.broadcasted_iota(jnp.int32, (count, width), 0) + start
        column = lax.broadcasted_iota(jnp.int32, (count, width), 1) + keys.start
        visible = (okey_v[0:1, keys] < oquery_v[rows, :]) | (row == column)
        bias = jnp.where(visible, 0.0, -1e30)

        def score(head):
            return lax.dot_general(
                query_v[head // 2, rows, :],
                key_v[head, keys, :],
                (((1,), (1,)), ((), ())),
                preferred_element_type=F32,
            )

        def weigh(head, scores):
            scores = scores + bias
            top = jnp.max(scores, axis=-1, keepdims=True)
            if combine:
                top = jnp.maximum(top, top_v[head, rows, :])
            return top, jnp.exp(scores - top).astype(BF16)

        def total(head, top, weights):
            part = jnp.dot(weights, value_v[head, keys, :], preferred_element_type=F32)
            if combine:
                part = part + part_v[head, rows, :] * jnp.exp(top_v[head, rows, :] - top)
            return part

        tops, parts = [], []
        ahead = score(0)
        behind = None
        for head in range(4):
            scores = ahead
            if head < 3:
                ahead = score(head + 1)
            top, weights = weigh(head, scores)
            if behind is not None:
                parts.append(total(head - 1, *behind))
            behind = (top, weights)
            tops.append(top)
        parts.append(total(3, *behind))
        return tops, parts

    def store(start, count, parts):
        half = lax.broadcasted_iota(jnp.int32, (count, 128), 1) < 64
        for pair in range(2):
            even, odd = parts[2 * pair : 2 * pair + 2]
            summed = jnp.where(half, even, odd)
            over = pltpu.roll(jnp.where(half, odd, even), 64, 1)
            att_v[pl.ds(start, count), pair * 128 : pair * 128 + 128] = (summed / over).astype(BF16)

    def send_home(piece, first_home, count):
        def one(peer, carry):
            home = first_home + lax.rem(me + peer + 1, count)

            @pl.when(home != me)
            def _():
                give_far(piece, home).start()

            @pl.when(home == me)
            def _():
                give_here(piece).start()

            return carry

        lax.fori_loop(0, count, one, 0)

    relay(0)
    project(0)

    def early(index, carry):
        start = pl.multiple_of(index * QUERIES, QUERIES)
        tops, parts = heads(start, QUERIES, slice(0, SPAN), False)
        for head in range(4):
            top_v[head, pl.ds(start, QUERIES), :] = tops[head]
            part_v[head, pl.ds(start, QUERIES), :] = parts[head]
        return carry

    lax.fori_loop(0, SPAN // QUERIES, early, 0)
    relay(1)
    project(1)

    @pl.when((tm > 0) & (tm < n_tm - 1))
    def _():
        for piece in range(PIECES):
            shift(piece).wait_send()

    for piece in range(PIECES):
        spreaded(piece).wait_send()
        relayed(piece).wait_send()

    def late(index, carry):
        start = pl.multiple_of(index * QUERIES, QUERIES)
        tops, parts = heads(start, QUERIES, slice(SPAN, 2 * SPAN), True)
        store(start, QUERIES, parts)
        send_home(0, index * HOMES, HOMES)
        return carry

    lax.fori_loop(0, SPAN // QUERIES, late, 0)

    def attend(index, carry):
        start = pl.multiple_of(SPAN + index * QUERIES, QUERIES)
        tops, parts = heads(start, QUERIES, slice(0, 2 * SPAN), False)
        store(start, QUERIES, parts)
        send_home(1, index * HOMES, HOMES)
        return carry

    lax.fori_loop(0, SPAN // QUERIES, attend, 0)

    loads[6].wait()
    def gather_home(piece, carry):
        give_here(piece).wait()

        returned(piece).wait_recv()
        returned(piece).wait_send()
        attended = jnp.concatenate(
            [back_v[piece, quarter].reshape(4 * PIECE, COLS) for quarter in range(4)], axis=1
        )
        projected = jnp.dot(attended, wo_v[...], preferred_element_type=F32)
        done = (second_v[piece].astype(F32) + projected).astype(BF16)
        for step in range(4):
            result[step, pl.ds(pl.multiple_of(piece * PIECE, PIECE), PIECE), :] = done[
                step * PIECE : (step + 1) * PIECE
            ]
        return carry

    lax.fori_loop(0, PIECES, gather_home, 0)


def per_device(
    tokens,
    conv_taps,
    norm_first,
    norm_second,
    norm_third,
    w_in,
    w_out,
    w_query,
    w_key,
    w_value,
    w_output,
    agent_order,
    present_steps,
):
    vmem, hbm = pl.BlockSpec(memory_space=pltpu.VMEM), pl.BlockSpec(memory_space=pl.ANY)
    dma = pltpu.SemaphoreType.DMA
    everyone = GROUP * ROWS
    return pl.pallas_call(
        block_kernel,
        out_shape=pltpu.VMEM(tokens.shape, BF16),
        in_specs=[hbm] * 11 + [vmem] * 2,
        out_specs=vmem,
        scratch_shapes=[
            pltpu.VMEM((5, WIDTH), F32),
            pltpu.VMEM((3, WIDTH), F32),
            pltpu.VMEM((8, 128), jnp.int32),
            pltpu.VMEM((WIDTH, HIDDEN), BF16),
            pltpu.VMEM((HIDDEN, WIDTH), BF16),
            pltpu.VMEM((3, WIDTH, COLS), BF16),
            pltpu.VMEM((WIDTH, WIDTH), BF16),
            pltpu.VMEM((4, ROWS, WIDTH), BF16),
            pltpu.VMEM((4, ROWS, WIDTH), BF16),
            pltpu.VMEM((8, PIECE, WIDTH), F32),
            pltpu.VMEM((4 * PIECE, WIDTH), BF16),
            pltpu.VMEM((4 * PIECE, HIDDEN), BF16),
            pltpu.VMEM((PIECES, 4 * PIECE, WIDTH), BF16),
            pltpu.VMEM((PIECES, 4, PIECE, WIDTH), BF16),
            pltpu.VMEM((PIECES, GROUP, PIECE, WIDTH), BF16),
            pltpu.VMEM((2, everyone, 128), BF16),
            pltpu.VMEM((4, everyone, 128), BF16),
            pltpu.VMEM((4, everyone, 128), BF16),
            pltpu.VMEM((everyone, COLS), BF16),
            pltpu.VMEM((PIECES, 4, 4, PIECE, COLS), BF16),
            pltpu.VMEM((GROUP, 8, 128), jnp.int32),
            pltpu.VMEM((8, everyone), F32),
            pltpu.VMEM((everyone, 1), F32),
            pltpu.VMEM((8, 128), jnp.int32),
            pltpu.VMEM((4, SPAN, 1), F32),
            pltpu.VMEM((4, SPAN, 128), F32),
            dma((4,)),
            dma((7,)),
            dma((PIECES,)),
            dma((PIECES,)),
            dma((PIECES,)),
            dma((PIECES,)),
            dma((1,)),
            dma((1,)),
            dma((PIECES,)),
            dma((PIECES * GROUP,)),
            dma((PIECES,)),
            dma((PIECES,)),
            dma((PIECES,)),
            dma((PIECES,)),
        ],
        compiler_params=pltpu.CompilerParams(
            collective_id=0, has_side_effects=True, vmem_limit_bytes=60 << 20
        ),
        name="space_time_block",
    )(
        tokens,
        conv_taps,
        norm_first.reshape(1, WIDTH),
        norm_second.reshape(1, WIDTH),
        norm_third.reshape(1, WIDTH),
        w_in,
        w_out,
        w_query,
        w_key,
        w_value,
        w_output,
        agent_order.reshape(1, ROWS),
        present_steps.reshape(1, ROWS),
    )


def solution(mesh):
    rows = P("tm", "agent", None)
    whole = P()
    return jax.shard_map(
        per_device,
        mesh=mesh,
        in_specs=(rows,) + (whole,) * 10 + (P("agent"), P("agent")),
        out_specs=rows,
        check_vma=False,
    )
```

```python
import functools

import jax
import jax.numpy as jnp
from jax import lax
from jax.experimental import pallas as pl
from jax.experimental.pallas import tpu as pltpu
from jax.sharding import PartitionSpec as P

EPS = 1e-05
HEADS = 16
MESH = pl.DeviceIdType.MESH
F32, BF16 = jnp.float32, jnp.bfloat16
GROUP = 16
ROWS = 64
WIDTH = 1024
HIDDEN = 3072
COLS = 256
FF_TILE = 1024
PIECES = 2
PIECE = ROWS // PIECES
SPAN = GROUP * PIECE
QUERIES = 256
HOMES = QUERIES // PIECE
SENDS = ((2, 1), (1, 1), (3, 1), (2, 0), (0, 1), (1, 0), (3, 0))


def remote(src, dst, send, recv, tm, agent):
    return pltpu.make_async_remote_copy(
        src_ref=src,
        dst_ref=dst,
        send_sem=send,
        recv_sem=recv,
        device_id=(tm, agent),
        device_id_type=MESH,
    )


def normed(rows, gain):
    scale = lax.rsqrt(jnp.mean(rows * rows, axis=-1, keepdims=True) + EPS)
    return rows * scale * gain


def block_kernel(
    tokens,
    taps_in,
    gain_first,
    gain_second,
    gain_third,
    w_in,
    w_out,
    w_query,
    w_key,
    w_value,
    w_output,
    order_own,
    present_own,
    result,
    taps,
    gains_v,
    own_v,
    win_v,
    wout_v,
    wqkv_v,
    wo_v,
    tok_v,
    prev_v,
    norm_v,
    inner_v,
    hid_v,
    second_v,
    mine_v,
    gath_v,
    query_v,
    key_v,
    value_v,
    att_v,
    back_v,
    info_v,
    okey_v,
    oquery_v,
    keep_v,
    top_v,
    part_v,
    small_sem,
    local_sem,
    keep_sem,
    here_sem,
    shift_send,
    shift_recv,
    info_send,
    info_recv,
    ex_send,
    ex_recv,
    rel_send,
    rel_recv,
    ret_send,
    ret_recv,
):
    tm, me = lax.axis_index("tm"), lax.axis_index("agent")
    n_tm = lax.axis_size("tm")
    z, x, core = me // 4, lax.rem(me // 2, 2), lax.rem(me, 2)
    group = lax.rem(me, 4)
    sibling = me + 1 - 2 * core
    after, before = lax.rem(tm + 1, n_tm), lax.rem(tm + n_tm - 1, n_tm)

    cols = pl.ds(pl.multiple_of(group * COLS, COLS), COLS)
    small = [
        pltpu.make_async_copy(taps_in, taps, small_sem.at[0]),
        pltpu.make_async_copy(gain_first, gains_v.at[0:1], small_sem.at[1]),
        pltpu.make_async_copy(gain_second, gains_v.at[1:2], small_sem.at[2]),
        pltpu.make_async_copy(gain_third, gains_v.at[2:3], small_sem.at[3]),
    ]
    loads = [
        pltpu.make_async_copy(tokens, tok_v, local_sem.at[0]),
        pltpu.make_async_copy(w_in, win_v, local_sem.at[1]),
        pltpu.make_async_copy(w_out, wout_v, local_sem.at[2]),
        pltpu.make_async_copy(w_query.at[:, cols], wqkv_v.at[0], local_sem.at[3]),
        pltpu.make_async_copy(w_key.at[:, cols], wqkv_v.at[1], local_sem.at[4]),
        pltpu.make_async_copy(w_value.at[:, cols], wqkv_v.at[2], local_sem.at[5]),
        pltpu.make_async_copy(w_output, wo_v, local_sem.at[6]),
    ]
    barrier = pltpu.get_barrier_semaphore()

    def greet(d, carry):
        pl.semaphore_signal(
            barrier, inc=1, device_id=(tm, lax.rem(me + d, GROUP)), device_id_type=MESH
        )
        return carry

    @pl.when(tm > 0)
    def _():
        pl.semaphore_signal(barrier, inc=1, device_id=(before, me), device_id_type=MESH)

    lax.fori_loop(1, GROUP, greet, 0)
    own_v[...] = jnp.zeros_like(own_v)
    for load in small + loads:
        load.start()
    own_v[0:1, 0:ROWS] = order_own[...]
    own_v[1:2, 0:ROWS] = present_own[...]

    band = lax.rem(lax.broadcasted_iota(jnp.int32, (1, 128), 1) // PIECE, PIECES)
    for number in range(2):
        once = own_v[number : number + 1, :]
        row = once + pltpu.roll(once, ROWS, 1)
        turned = [row] + [pltpu.roll(row, PIECE * i, 1) for i in range(1, PIECES)]
        for piece in range(PIECES):
            picked = row
            for i in range(1, PIECES):
                picked = jnp.where(lax.rem(band + PIECES - i, PIECES) == piece, turned[i], picked)
            keep_v[number * PIECES + piece : number * PIECES + piece + 1, :] = picked
    info_v[me] = keep_v[...]

    @pl.when(tm < n_tm - 1)
    def _():
        pl.semaphore_wait(barrier, GROUP)

    @pl.when(tm == n_tm - 1)
    def _():
        pl.semaphore_wait(barrier, GROUP - 1)


    def shift(piece):
        rows = pl.ds(pl.multiple_of(piece * PIECE, PIECE), PIECE)
        return remote(
            tokens.at[:, rows, :],
            prev_v.at[:, rows, :],
            shift_send.at[piece],
            shift_recv.at[piece],
            after,
            me,
        )

    def info_copy(slot, peer):
        return remote(
            info_v.at[me], info_v.at[slot], info_send.at[0], info_recv.at[0], tm, peer
        )

    def tell(d, carry):
        info_copy(me, lax.rem(me + d, GROUP)).start()
        return carry

    lax.fori_loop(1, GROUP, tell, 0)

    @pl.when(tm < n_tm - 1)
    def _():
        for piece in range(PIECES):
            shift(piece).start()

    @pl.when(tm == 0)
    def _():
        def clear(i, carry):
            prev_v[i // 4, pl.ds(pl.multiple_of(lax.rem(i, 4) * 16, 16), 16), :] = jnp.zeros(
                (16, WIDTH), BF16
            )
            return carry

        lax.fori_loop(0, ROWS // 4, clear, 0)

    for load in small:
        load.wait()
    gain1, gain2, gain3 = gains_v[0:1], gains_v[1:2], gains_v[2:3]
    loads[0].wait()

    def feed(piece):
        rows = pl.ds(pl.multiple_of(piece * PIECE, PIECE), PIECE)
        for step in range(4):
            norm_v[4 + step] = normed(tok_v[step, rows].astype(F32), gain1)

        @pl.when(tm > 0)
        def _():
            shift(piece).wait_recv()

        for step in range(4):
            norm_v[step] = normed(prev_v[step, rows].astype(F32), gain1)
        firsts = []
        for step in range(4):
            mixed = taps[0:1, :] * norm_v[step + 4]
            for lag in range(1, 5):
                mixed = mixed + taps[lag : lag + 1, :] * norm_v[step + 4 - lag]
            firsts.append((tok_v[step, rows].astype(F32) + mixed).astype(BF16))
        first = jnp.concatenate(firsts, axis=0)
        second_v[piece] = first
        inner = normed(first.astype(F32), gain2).astype(BF16)
        inner_v[...] = inner

        def hidden(tile, carry):
            across = pl.ds(pl.multiple_of(tile * FF_TILE, FF_TILE), FF_TILE)
            pre = jnp.dot(inner_v[...], win_v[:, across], preferred_element_type=F32)
            act = 0.5 * pre * (1.0 + lax.erf(pre * 0.7071067811865476))
            hid_v[:, across] = act.astype(BF16)
            return carry

        lax.fori_loop(0, HIDDEN // FF_TILE, hidden, 0)
        ffn = jnp.dot(hid_v[...], wout_v[...], preferred_element_type=F32)
        second = (second_v[piece].astype(F32) + ffn).astype(BF16)
        second_v[piece] = second
        attn_in = normed(second.astype(F32), gain3).astype(BF16)
        for step in range(4):
            mine_v[piece, step] = attn_in[step * PIECE : (step + 1) * PIECE]

    def to_step(piece, turn, other):
        step = lax.rem(z + turn, 4)
        return remote(
            mine_v.at[piece, step],
            gath_v.at[piece, me],
            ex_send.at[piece],
            ex_recv.at[piece * GROUP + me],
            tm,
            step * 4 + 2 * ((1 - x) if other else x) + core,
        )

    def keep(piece):
        return pltpu.make_async_copy(
            mine_v.at[piece, z], gath_v.at[piece, me], keep_sem.at[piece]
        )

    def own_to_sibling(piece):
        return remote(
            mine_v.at[piece, z],
            gath_v.at[piece, me],
            rel_send.at[piece],
            rel_recv.at[piece],
            tm,
            sibling,
        )

    def spread(piece):
        @pl.when(tm == 0)
        def _():
            shift(piece).wait_send()

        keep(piece).start()
        own_to_sibling(piece).start()
        for turn, other in SENDS:
            to_step(piece, turn, other).start()


    def forward(piece, slot):
        return remote(
            gath_v.at[piece, slot],
            gath_v.at[piece, slot],
            rel_send.at[piece],
            rel_recv.at[piece],
            tm,
            sibling,
        )

    def others():
        return [
            lax.rem(z + 4 - turn, 4) * 4 + 2 * ((1 - x) if other else x) + core
            for turn, other in SENDS
        ]

    def relay(piece):
        for slot in others():
            remote(
                mine_v.at[piece, 0],
                gath_v.at[piece, slot],
                ex_send.at[0],
                ex_recv.at[piece * GROUP + slot],
                tm,
                slot,
            ).wait_recv()
            forward(piece, slot).start()

    def relayed(piece):
        eight = gath_v.at[piece, pl.ds(0, GROUP // 2)]
        return remote(eight, eight, rel_send.at[piece], rel_recv.at[piece], tm, sibling)

    def spreaded(piece):
        seven = gath_v.at[piece, pl.ds(0, len(SENDS))]
        return remote(seven, seven, ex_send.at[piece], rel_recv.at[piece], tm, sibling)

    lane = lax.broadcasted_iota(jnp.int32, (SPAN, 128), 1) < 64

    def project(piece):
        relayed(piece).wait_recv()
        keep(piece).wait()
        rows = pl.ds(pl.multiple_of(piece * SPAN, SPAN), SPAN)
        source = gath_v[piece].reshape(SPAN, WIDTH)
        query = jnp.dot(source, wqkv_v[0], preferred_element_type=F32) * 0.125
        key = jnp.dot(source, wqkv_v[1], preferred_element_type=F32)
        value = jnp.dot(source, wqkv_v[2], preferred_element_type=F32)
        for pair in range(2):
            span = slice(pair * 128, pair * 128 + 128)
            query_v[pair, rows, :] = query[:, span].astype(BF16)
            key_v[2 * pair, rows, :] = jnp.where(lane, key[:, span], 0.0).astype(BF16)
            key_v[2 * pair + 1, rows, :] = jnp.where(lane, 0.0, key[:, span]).astype(BF16)
            value_v[2 * pair, rows, :] = jnp.where(lane, value[:, span], 1.0).astype(BF16)
            value_v[2 * pair + 1, rows, :] = jnp.where(lane, 1.0, value[:, span]).astype(BF16)

    def places():
        told = info_v.at[pl.ds(0, GROUP - 1)]
        both = remote(told, told, info_send.at[0], info_recv.at[0], tm, sibling)
        both.wait_recv()
        both.wait_send()
        now = tm * 4 + z
        eye = lax.broadcasted_iota(jnp.int32, (128, 128), 0) == lax.broadcasted_iota(
            jnp.int32, (128, 128), 1
        )
        part = lax.broadcasted_iota(jnp.int32, (1, 128), 1) // PIECE
        several = 128 // PIECE
        for piece in range(PIECES):
            for bunch in range(GROUP // several):
                place = info_v[bunch * several, piece : piece + 1]
                until = info_v[bunch * several, PIECES + piece : PIECES + piece + 1]
                for i in range(1, several):
                    tile = bunch * several + i
                    place = jnp.where(part == i, info_v[tile, piece : piece + 1], place)
                    until = jnp.where(
                        part == i, info_v[tile, PIECES + piece : PIECES + piece + 1], until
                    )
                place_f = place.astype(F32)
                start = piece * SPAN + bunch * 128
                okey_v[0:1, start : start + 128] = jnp.where(now < until, place_f, 1e9)
                oquery_v[start : start + 128, :] = jnp.sum(
                    jnp.where(eye, jnp.broadcast_to(place_f, (128, 128)), 0.0),
                    axis=1,
                    keepdims=True,
                )

    places()
    for load in loads[1:6]:
        load.wait()

    def produce(piece, carry):
        feed(piece)
        spread(piece)
        return carry

    lax.fori_loop(0, PIECES, produce, 0)


    def give(piece, home):
        return (
            att_v.at[pl.ds(pl.multiple_of(piece * SPAN + home * PIECE, PIECE), PIECE), :],
            back_v.at[piece, group, z],
        )

    def give_far(piece, home):
        source, target = give(piece, home)
        return remote(
            source,
            target,
            ret_send.at[piece],
            ret_recv.at[piece],
            tm,
            home,
        )

    def returned(piece):
        fifteen = att_v.at[pl.ds(0, (GROUP - 1) * PIECE), :]
        return remote(fifteen, fifteen, ret_send.at[piece], ret_recv.at[piece], tm, sibling)

    def give_here(piece):
        source, target = give(piece, me)
        return pltpu.make_async_copy(source, target, here_sem.at[piece])

    def heads(start, count, keys, combine):
        rows = pl.ds(start, count)
        width = keys.stop - keys.start
        row = lax.broadcasted_iota(jnp.int32, (count, width), 0) + start
        column = lax.broadcasted_iota(jnp.int32, (count, width), 1) + keys.start
        visible = (okey_v[0:1, keys] < oquery_v[rows, :]) | (row == column)
        bias = jnp.where(visible, 0.0, -1e30)

        def score(head):
            return lax.dot_general(
                query_v[head // 2, rows, :],
                key_v[head, keys, :],
                (((1,), (1,)), ((), ())),
                preferred_element_type=F32,
            )

        def weigh(head, scores):
            scores = scores + bias
            top = jnp.max(scores, axis=-1, keepdims=True)
            if combine:
                top = jnp.maximum(top, top_v[head, rows, :])
            return top, jnp.exp(scores - top).astype(BF16)

        def total(head, top, weights):
            part = jnp.dot(weights, value_v[head, keys, :], preferred_element_type=F32)
            if combine:
                part = part + part_v[head, rows, :] * jnp.exp(top_v[head, rows, :] - top)
            return part

        tops, parts = [], []
        ahead = score(0)
        behind = None
        for head in range(4):
            scores = ahead
            if head < 3:
                ahead = score(head + 1)
            top, weights = weigh(head, scores)
            if behind is not None:
                parts.append(total(head - 1, *behind))
            behind = (top, weights)
            tops.append(top)
        parts.append(total(3, *behind))
        return tops, parts

    def store(start, count, parts):
        half = lax.broadcasted_iota(jnp.int32, (count, 128), 1) < 64
        for pair in range(2):
            even, odd = parts[2 * pair : 2 * pair + 2]
            summed = jnp.where(half, even, odd)
            over = pltpu.roll(jnp.where(half, odd, even), 64, 1)
            att_v[pl.ds(start, count), pair * 128 : pair * 128 + 128] = (summed / over).astype(BF16)

    def send_home(piece, first_home, count):
        def one(peer, carry):
            home = first_home + lax.rem(me + peer + 1, count)

            @pl.when(home != me)
            def _():
                give_far(piece, home).start()

            @pl.when(home == me)
            def _():
                give_here(piece).start()

            return carry

        lax.fori_loop(0, count, one, 0)

    relay(0)
    project(0)

    def early(index, carry):
        start = pl.multiple_of(index * QUERIES, QUERIES)
        tops, parts = heads(start, QUERIES, slice(0, SPAN), False)
        for head in range(4):
            top_v[head, pl.ds(start, QUERIES), :] = tops[head]
            part_v[head, pl.ds(start, QUERIES), :] = parts[head]
        return carry

    lax.fori_loop(0, SPAN // QUERIES, early, 0)
    relay(1)
    project(1)

    @pl.when((tm > 0) & (tm < n_tm - 1))
    def _():
        for piece in range(PIECES):
            shift(piece).wait_send()

    for piece in range(PIECES):
        spreaded(piece).wait_send()
        relayed(piece).wait_send()

    def late(index, carry):
        start = pl.multiple_of(index * QUERIES, QUERIES)
        tops, parts = heads(start, QUERIES, slice(SPAN, 2 * SPAN), True)
        store(start, QUERIES, parts)
        send_home(0, index * HOMES, HOMES)
        return carry

    lax.fori_loop(0, SPAN // QUERIES, late, 0)

    def attend(index, carry):
        start = pl.multiple_of(SPAN + index * QUERIES, QUERIES)
        tops, parts = heads(start, QUERIES, slice(0, 2 * SPAN), False)
        store(start, QUERIES, parts)
        send_home(1, index * HOMES, HOMES)
        return carry

    lax.fori_loop(0, SPAN // QUERIES, attend, 0)

    loads[6].wait()
    def gather_home(piece, carry):
        give_here(piece).wait()

        returned(piece).wait_recv()
        returned(piece).wait_send()
        attended = jnp.concatenate(
            [back_v[piece, quarter].reshape(4 * PIECE, COLS) for quarter in range(4)], axis=1
        )
        projected = jnp.dot(attended, wo_v[...], preferred_element_type=F32)
        done = (second_v[piece].astype(F32) + projected).astype(BF16)
        for step in range(4):
            result[step, pl.ds(pl.multiple_of(piece * PIECE, PIECE), PIECE), :] = done[
                step * PIECE : (step + 1) * PIECE
            ]
        return carry

    lax.fori_loop(0, PIECES, gather_home, 0)


def per_device(
    tokens,
    conv_taps,
    norm_first,
    norm_second,
    norm_third,
    w_in,
    w_out,
    w_query,
    w_key,
    w_value,
    w_output,
    agent_order,
    present_steps,
):
    vmem, hbm = pl.BlockSpec(memory_space=pltpu.VMEM), pl.BlockSpec(memory_space=pl.ANY)
    dma = pltpu.SemaphoreType.DMA
    everyone = GROUP * ROWS
    return pl.pallas_call(
        block_kernel,
        out_shape=pltpu.VMEM(tokens.shape, BF16),
        in_specs=[hbm] * 11 + [vmem] * 2,
        out_specs=vmem,
        scratch_shapes=[
            pltpu.VMEM((5, WIDTH), F32),
            pltpu.VMEM((3, WIDTH), F32),
            pltpu.VMEM((8, 128), jnp.int32),
            pltpu.VMEM((WIDTH, HIDDEN), BF16),
            pltpu.VMEM((HIDDEN, WIDTH), BF16),
            pltpu.VMEM((3, WIDTH, COLS), BF16),
            pltpu.VMEM((WIDTH, WIDTH), BF16),
            pltpu.VMEM((4, ROWS, WIDTH), BF16),
            pltpu.VMEM((4, ROWS, WIDTH), BF16),
            pltpu.VMEM((8, PIECE, WIDTH), F32),
            pltpu.VMEM((4 * PIECE, WIDTH), BF16),
            pltpu.VMEM((4 * PIECE, HIDDEN), BF16),
            pltpu.VMEM((PIECES, 4 * PIECE, WIDTH), BF16),
            pltpu.VMEM((PIECES, 4, PIECE, WIDTH), BF16),
            pltpu.VMEM((PIECES, GROUP, PIECE, WIDTH), BF16),
            pltpu.VMEM((2, everyone, 128), BF16),
            pltpu.VMEM((4, everyone, 128), BF16),
            pltpu.VMEM((4, everyone, 128), BF16),
            pltpu.VMEM((everyone, COLS), BF16),
            pltpu.VMEM((PIECES, 4, 4, PIECE, COLS), BF16),
            pltpu.VMEM((GROUP, 8, 128), jnp.int32),
            pltpu.VMEM((8, everyone), F32),
            pltpu.VMEM((everyone, 1), F32),
            pltpu.VMEM((8, 128), jnp.int32),
            pltpu.VMEM((4, SPAN, 1), F32),
            pltpu.VMEM((4, SPAN, 128), F32),
            dma((4,)),
            dma((7,)),
            dma((PIECES,)),
            dma((PIECES,)),
            dma((PIECES,)),
            dma((PIECES,)),
            dma((1,)),
            dma((1,)),
            dma((PIECES,)),
            dma((PIECES * GROUP,)),
            dma((PIECES,)),
            dma((PIECES,)),
            dma((PIECES,)),
            dma((PIECES,)),
        ],
        compiler_params=pltpu.CompilerParams(
            collective_id=0, has_side_effects=True, vmem_limit_bytes=60 << 20
        ),
        name="space_time_block",
    )(
        tokens,
        conv_taps,
        norm_first.reshape(1, WIDTH),
        norm_second.reshape(1, WIDTH),
        norm_third.reshape(1, WIDTH),
        w_in,
        w_out,
        w_query,
        w_key,
        w_value,
        w_output,
        agent_order.reshape(1, ROWS),
        present_steps.reshape(1, ROWS),
    )


def solution(mesh):
    rows = P("tm", "agent", None)
    whole = P()
    return jax.shard_map(
        per_device,
        mesh=mesh,
        in_specs=(rows,) + (whole,) * 10 + (P("agent"), P("agent")),
        out_specs=rows,
        check_vma=False,
    )
```
